512 devices in a mesh: seq: 64 (over z, x, core), head: 8 (over y).
Axes of the slice: x: 4, y: 8, z: 8, core: 2. Of those that a mesh axis runs over, the one named last changes fastest.
Arguments:
- queries: bfloat16 [65536, 4096], P('seq', 'head'), may hold values from -0.5 to 0.5
- key_rows: bfloat16 [65536, 4096], P('seq', 'head'), may hold values from -6 to 6
- value_rows: bfloat16 [65536, 4096], P('seq', 'head'), may hold values from -6 to 6
- decay_rates: float32 [32], P('head'), as said below
- out_gain: float32 [4096], P('head'), may hold values from 0.5 to 1.5
Outputs:
- attended: bfloat16 [65536, 4096], P('seq', 'head')
The draws below stay inside these ranges and needn't reach their ends.
Inputs may be any that keep to these rules, and one draw needn't show every extreme that they name: `decay_rates`: positive per-head decay rates.
All inputs are finite; a program needn't handle non-finite values.
Results may differ from the reference program's by a relative error of at most 0.0054.
Values sent between devices are 32-bit elements; how exact they have to be, the bound alone decides.
No kernel may reach another device: no remote copies, remote signals or barrier semaphores. Data moves between devices by JAX's collectives and lax.ppermute only.
A program may use at most 64 MiB of HBM per device.

```python
import jax
import jax.numpy as jnp
from jax import lax

H = 32
E = 128
BLOCK = 256
TOKENS = 65536
BLOCKS = 256


def draw_decay_rates(key, part):
    order_key = jax.random.fold_in(key, 11)
    slow_key = jax.random.fold_in(key, 12)
    fast_key = jax.random.fold_in(key, 13)
    head_ranks = jax.random.permutation(order_key, H)
    slow_heads = head_ranks < H // 2
    slow_rate = jnp.exp(jax.random.uniform(slow_key, (H,), jnp.float32, jnp.log(0.25), jnp.log(2.0))) / TOKENS
    fast_rate = jnp.exp(jax.random.uniform(fast_key, (H,), jnp.float32, jnp.log(1.0 / 50.0), jnp.log(1.0 / 30.0)))
    return jnp.where(slow_heads, slow_rate, fast_rate).astype(jnp.float32)


def block_scale(stream_key, extent, cuts, low, top_value):
    def one(dim, shards_of):
        heights = jax.random.uniform(jax.random.fold_in(jax.random.fold_in(stream_key, 6), dim), (shards_of,), jnp.float32, low / len(cuts), top_value / len(cuts))
        return jnp.repeat(jnp.exp(heights), extent[dim] // shards_of).reshape((-1,) + (1,) * (len(extent) - dim - 1))

    gain = one(*cuts[0])
    for cut in cuts[1:]:
        gain = gain * one(*cut)
    return gain


def noise(own_key, shape, spread, most, split=(), held_as=jnp.bfloat16):
    entries = spread * jax.random.normal(own_key, shape, jnp.float32)
    if split:
        entries = entries * block_scale(own_key, shape, split, -0.22, 0.18)
    return jnp.clip(entries, -most, most).astype(held_as)


def setup_inputs(seed: int = 0) -> dict:
    arg_keys = jax.random.split(jax.random.key(seed), 6)
    return {
        "queries": noise(arg_keys[0], (TOKENS, H * E), E ** -0.5, 0.5, ((0, 64), (1, 8))),
        "key_rows": noise(arg_keys[1], (TOKENS, H * E), 1.0, 6.0, ((0, 64), (1, 8))),
        "value_rows": noise(arg_keys[2], (TOKENS, H * E), 1.0, 6.0, ((0, 64), (1, 8))),
        "decay_rates": draw_decay_rates(jax.random.fold_in(arg_keys[5], 71), 0),
        "out_gain": jnp.clip(1.0 + 0.1 * jax.random.normal(arg_keys[4], (H * E,), jnp.float32), 0.5, 1.5),
    }


EPSILON = 1e-06

def to_half(value_matrix):
    return lax.optimization_barrier(value_matrix.astype(jnp.bfloat16)).astype(jnp.float32)

def reference(queries, key_rows, value_rows, decay_rates, out_gain):
    log_decay = -decay_rates.astype(jnp.float32)
    positions = jnp.arange(BLOCK).astype(jnp.float32)
    distance = positions[:, None] - positions[None, :]
    masked = jnp.where(distance[None] >= 0, jnp.exp(log_decay[:, None, None] * jnp.maximum(distance, 0.0)[None]), 0.0)
    key_scale = jnp.exp(log_decay[None, :] * (BLOCK - 1 - positions)[:, None])
    query_scale = jnp.exp(log_decay[None, :] * (positions + 1.0)[:, None])
    block_decay = jnp.exp(log_decay * BLOCK)
    gain_heads = out_gain.reshape(H, E).astype(jnp.float32)
    shaped = (queries.reshape(BLOCKS, BLOCK, H, E), key_rows.reshape(BLOCKS, BLOCK, H, E), value_rows.reshape(BLOCKS, BLOCK, H, E))

    def block_step(carry_state, block):
        query_block = block[0].astype(jnp.float32)
        key_block = block[1].astype(jnp.float32)
        current_value_block = block[2].astype(jnp.float32)
        scores = jnp.einsum('qhe,khe->hqk', query_block, key_block)
        local_out = jnp.einsum('hqk,khe->qhe', to_half(scores * masked), current_value_block)
        carried_out = jnp.einsum('qhe,hef->qhf', query_block, to_half(carry_state)) * query_scale[:, :, None]
        mixed = local_out + carried_out
        decay_scaled_keys = to_half(key_block * key_scale[:, :, None])
        per_block_state = jnp.einsum('tap,tax->apx', decay_scaled_keys, current_value_block)
        next_state = block_decay[:, None, None] * carry_state + per_block_state
        inverse = lax.rsqrt(lax.optimization_barrier(jnp.mean(mixed * mixed, axis=(1, 2))) + EPSILON)
        attended = (mixed * inverse[:, None, None] * gain_heads[None]).astype(jnp.bfloat16)
        return (next_state, attended)
    initial_state = jnp.zeros((H, E, E), jnp.float32)
    _, outputs = lax.scan(block_step, initial_state, shaped)
    return outputs.reshape(TOKENS, H * E)
```

```python
import functools

import jax
import jax.numpy as jnp
from jax import lax
from jax.experimental import pallas as pl
from jax.experimental.pallas import tpu as pltpu
from jax.sharding import Mesh
from jax.sharding import PartitionSpec as P

H = 32
E = 128
BLOCK = 256
EPSILON = 1e-06
SEQ = ("z", "x", "c")
CHIPS = ("z", "x")
HEAD = "head"

F32 = jnp.float32
BF16 = jnp.bfloat16
VMEM = pl.BlockSpec(memory_space=pltpu.VMEM)
SMEM = pl.BlockSpec(memory_space=pltpu.SMEM)
HBM = pl.BlockSpec(memory_space=pl.ANY)


def call(kernel, outs, ins, out_specs, scratch=(), limit=24, flops=0, moved=0, name=None):
    return pl.pallas_call(
        kernel,
        out_shape=outs,
        in_specs=ins,
        out_specs=out_specs,
        scratch_shapes=list(scratch),
        compiler_params=pltpu.CompilerParams(vmem_limit_bytes=limit << 20),
        cost_estimate=pl.CostEstimate(flops=flops, bytes_accessed=moved, transcendentals=0),
        name=name,
    )


def power(rate, distance):
    return jnp.exp(-rate * distance)


def head_columns(h):
    return slice(h * E, (h + 1) * E)


def states_kernel(count, heads, rates, keys_hbm, values_hbm, state, before, keys, values, sems):
    def copies(b):
        rows = pl.ds(b * BLOCK, BLOCK)
        return (
            pltpu.make_async_copy(keys_hbm.at[rows], keys.at[rows], sems.at[0, b]),
            pltpu.make_async_copy(values_hbm.at[rows], values.at[rows], sems.at[1, b]),
        )

    for b in range(count):
        for copy in copies(b):
            copy.start()
    inner = lax.broadcasted_iota(jnp.int32, (BLOCK, E), 0).astype(F32)
    for b in range(count):
        rows = pl.ds(b * BLOCK, BLOCK)
        for copy in copies(b):
            copy.wait()
        for h in range(heads):
            rate = rates[h]
            scaled = keys[rows, head_columns(h)].astype(F32) * power(rate, BLOCK - 1.0 - inner)
            block = lax.dot_general(
                scaled.astype(BF16),
                values[rows, head_columns(h)],
                (((0,), (0,)), ((), ())),
                preferred_element_type=F32,
            )
            if b > 0:
                previous = state[h]
                before[b - 1, h] = previous
                block = previous * power(jnp.full((E, E), rate, F32), float(BLOCK)) + block
            state[h] = block


def chip_kernel(length, half, rates, both, total):
    first = lax.axis_index("c") * half
    for i in range(half):
        decay = power(jnp.full((E, E), rates[first + i], F32), float(length))
        total[i] = both[0, first + i] * decay + both[1, first + i]


def scan_kernel(length, half, chips, rates, totals, prefixes):
    piece = lax.axis_index("z") * lax.axis_size("x") + lax.axis_index("x")
    h = lax.axis_index("c") * half + piece // (chips // half)
    decay = power(jnp.full(totals.shape[1:], rates[h], F32), 2.0 * length)
    running = jnp.zeros(totals.shape[1:], F32)
    for i in range(chips):
        prefixes[i] = running
        running = running * decay + totals[i]


def local_kernel(count, heads, rates, queries, keys, values, local):
    row = lax.broadcasted_iota(jnp.int32, (BLOCK, BLOCK), 0)
    column = lax.broadcasted_iota(jnp.int32, (BLOCK, BLOCK), 1)
    distance = (row - column).astype(F32)
    for h in range(heads):
        masked = jnp.where(distance >= 0, power(rates[h], jnp.maximum(distance, 0.0)), 0.0)
        for b in range(count):
            rows = pl.ds(b * BLOCK, BLOCK)
            scores = lax.dot_general(
                queries[rows, head_columns(h)],
                keys[rows, head_columns(h)],
                (((1,), (1,)), ((), ())),
                preferred_element_type=F32,
            )
            weights = (scores * masked).astype(BF16)
            local[rows, head_columns(h)] = jnp.dot(
                weights, values[rows, head_columns(h)], preferred_element_type=F32
            )


def mix_kernel(count, heads, rates, queries, local, prefix, both, before, mixed, squares):
    length = float(count * BLOCK)
    second = lax.axis_index("c") == 1
    inner = lax.broadcasted_iota(jnp.int32, (BLOCK, E), 0).astype(F32)
    entering = []
    for h in range(heads):
        decayed = prefix[h] * power(jnp.full((E, E), rates[h], F32), length) + both[0, h]
        entering.append(jnp.where(second, decayed, prefix[h]))
    for b in range(count):
        rows = pl.ds(b * BLOCK, BLOCK)
        total = jnp.zeros((BLOCK, E), F32)
        for h in range(heads):
            carried = entering[h]
            if b > 0:
                decay = power(jnp.full((E, E), rates[h], F32), float(b * BLOCK))
                carried = carried * decay + before[b - 1, h]
            out = jnp.dot(
                queries[rows, head_columns(h)], carried.astype(BF16), preferred_element_type=F32
            )
            out = local[rows, head_columns(h)] + out * power(rates[h], inner + 1.0)
            mixed[rows, head_columns(h)] = out
            total = total + out * out
        sums = lax.dot_general(
            jnp.ones((8, E), F32),
            total,
            (((1,), (1,)), ((), ())),
            precision=lax.Precision.HIGHEST,
            preferred_element_type=F32,
        )
        for r in range(BLOCK // E):
            row = jnp.broadcast_to(sums[0:1, r * E : (r + 1) * E], (squares.shape[0], E))
            squares[:, b * (BLOCK // E) + r, :] = row


def norm_kernel(count, mixed, squares, gain, out_hbm, out, sems):
    sums = squares[0]
    for i in range(1, squares.shape[0]):
        sums = sums + squares[i]
    inverse = lax.rsqrt(sums / float(H * E) + EPSILON)
    tiles = out.shape[0] // E
    for t in range(tiles):
        rows = pl.ds(t * E, E)
        column = jnp.broadcast_to(inverse[t : t + 1, :], (E, E)).T
        for h in range(out.shape[1] // E):
            part = mixed[rows, head_columns(h)] * column * gain[:, head_columns(h)]
            out[rows, head_columns(h)] = part.astype(BF16)
        if t % 2 == 1:
            pair = pl.ds((t - 1) * E, 2 * E)
            pltpu.make_async_copy(out.at[pair], out_hbm.at[pair], sems.at[t // 2]).start()
    for t in range(1, tiles, 2):
        pair = pl.ds((t - 1) * E, 2 * E)
        pltpu.make_async_copy(out.at[pair], out_hbm.at[pair], sems.at[t // 2]).wait()


def body(queries, key_rows, value_rows, decay_rates, out_gain):
    length, width = queries.shape
    heads = decay_rates.shape[0]
    count = length // BLOCK
    half = heads // 2
    chips = lax.axis_size("z") * lax.axis_size("x")
    parts = lax.axis_size(HEAD)
    shape = jax.ShapeDtypeStruct

    state, before = call(
        functools.partial(states_kernel, count, heads),
        (shape((heads, E, E), F32), shape((count - 1, heads, E, E), F32)),
        [SMEM, HBM, HBM],
        (VMEM, VMEM),
        [
            pltpu.VMEM((length, width), BF16),
            pltpu.VMEM((length, width), BF16),
            pltpu.SemaphoreType.DMA((2, count)),
        ],
        flops=2 * length * E * width,
        moved=4 * length * width,
        name="states",
    )(decay_rates, key_rows, value_rows)
    both = lax.all_gather(state, "c")
    total = call(
        functools.partial(chip_kernel, length, half),
        shape((half, E, E), F32),
        [SMEM, VMEM],
        VMEM,
        name="chip",
    )(decay_rates, both)
    owned = lax.all_to_all(total.reshape(chips, -1, E), CHIPS, 0, 0, tiled=True)
    prefixes = call(
        functools.partial(scan_kernel, length, half, chips),
        shape(owned.shape, F32),
        [SMEM, VMEM],
        VMEM,
        name="scan",
    )(decay_rates, owned)
    mine = lax.all_to_all(prefixes, CHIPS, 0, 0, tiled=True).reshape(half, E, E)
    prefix = lax.all_gather(mine, "c", tiled=True)
    local = call(
        functools.partial(local_kernel, count, heads),
        shape((length, width), F32),
        [SMEM, VMEM, VMEM, VMEM],
        VMEM,
        flops=4 * length * BLOCK * width,
        moved=10 * length * width,
        name="local",
    )(decay_rates, queries, key_rows, value_rows)
    mixed, squares = call(
        functools.partial(mix_kernel, count, heads),
        (shape((length, width), F32), shape((parts, length // E, E), F32)),
        [SMEM, VMEM, VMEM, VMEM, VMEM, VMEM],
        (VMEM, VMEM),
        flops=2 * length * E * width,
        moved=10 * length * width,
        name="mix",
    )(decay_rates, queries, local, prefix, both, before)
    shared = lax.all_to_all(squares, HEAD, 0, 0, tiled=True)
    return call(
        functools.partial(norm_kernel, count),
        shape((length, width), BF16),
        [VMEM, VMEM, VMEM],
        HBM,
        [pltpu.VMEM((length, width), BF16), pltpu.SemaphoreType.DMA((count,))],
        moved=6 * length * width,
        name="norm",
    )(mixed, shared, out_gain.reshape(1, width))


def solution(mesh):
    torus = Mesh(mesh.devices.reshape(8, 4, 2, mesh.shape["head"]), ("z", "x", "c", "head"))
    in_specs = (P(SEQ, "head"), P(SEQ, "head"), P(SEQ, "head"), P("head"), P("head"))
    return jax.shard_map(
        body, mesh=torus, in_specs=in_specs, out_specs=P(SEQ, "head"), check_vma=False
    )
```

```python
import functools

import jax
import jax.numpy as jnp
from jax import lax
from jax.experimental import pallas as pl
from jax.experimental.pallas import tpu as pltpu
from jax.sharding import Mesh
from jax.sharding import PartitionSpec as P

H = 32
E = 128
BLOCK = 256
EPSILON = 1e-06
SEQ = ("z", "x", "c")
CHIPS = ("z", "x")
HEAD = "head"

F32 = jnp.float32
BF16 = jnp.bfloat16
VMEM_BYTES = 67043328
STATES_ROOM = 11 << 20
LOCAL_ROOM = 30 << 20
VMEM = pl.BlockSpec(memory_space=pltpu.VMEM)
HBM = pl.BlockSpec(memory_space=pltpu.HBM)


def call(kernel, outs, ins, out_specs, scratch=(), room=40 << 20, flops=0, moved=0, name=None):
    return pl.pallas_call(
        kernel,
        out_shape=outs,
        in_specs=ins,
        out_specs=out_specs,
        scratch_shapes=list(scratch),
        compiler_params=pltpu.CompilerParams(vmem_limit_bytes=VMEM_BYTES - room),
        cost_estimate=pl.CostEstimate(flops=flops, bytes_accessed=moved, transcendentals=0),
        name=name,
    )


def power(rate, distance):
    return jnp.exp(-rate * distance)


def head_columns(h):
    return slice(h * E, (h + 1) * E)


def states_kernel(
    count, heads, rates_hbm, keys_hbm, values_hbm, state, wide, keys, values, scale, rates, sems, rate_sem
):
    def copies(b):
        rows = pl.ds(b * BLOCK, BLOCK)
        return (
            pltpu.make_async_copy(keys_hbm.at[rows], keys.at[rows], sems.at[0, b]),
            pltpu.make_async_copy(values_hbm.at[rows], values.at[rows], sems.at[1, b]),
        )

    rate_copy = pltpu.make_async_copy(rates_hbm, rates, rate_sem)
    rate_copy.start()
    for b in range(count):
        for copy in copies(b):
            copy.start()
    inner = lax.broadcasted_iota(jnp.int32, (BLOCK, E), 0).astype(F32)
    rate_copy.wait()
    for h in range(heads):
        wide[h] = jnp.full((8, E), rates[h], F32)
        scale[h] = power(rates[h], BLOCK - 1.0 - inner)
    for b in range(count):
        rows = pl.ds(b * BLOCK, BLOCK)
        for copy in copies(b):
            copy.wait()
        for h in range(heads):
            scaled = keys[rows, head_columns(h)].astype(F32) * scale[h]
            block = lax.dot_general(
                scaled.astype(BF16),
                values[rows, head_columns(h)],
                (((0,), (0,)), ((), ())),
                preferred_element_type=F32,
            )
            if b > 0:
                block = state[h] * power(wide[h, 0:1], float(BLOCK)) + block
            state[h] = block


def chip_kernel(length, half, wide, both, total):
    first = lax.axis_index("c") * half
    for i in range(half):
        decay = power(wide[first + i, 0:1], float(length))
        total[i] = both[0, first + i] * decay + both[1, first + i]


def scan_kernel(length, half, chips, wide, totals, prefixes):
    piece = lax.axis_index("z") * lax.axis_size("x") + lax.axis_index("x")
    h = lax.axis_index("c") * half + piece // (chips // half)
    decay = power(wide[h], 2.0 * length)
    running = jnp.zeros(totals.shape[1:], F32)
    for i in range(chips):
        prefixes[i] = running
        running = running * decay + totals[i]


def two_halves(matrix):
    high = matrix.astype(BF16)
    low = (matrix - high.astype(F32)).astype(BF16)
    return jnp.concatenate([high, low], axis=0)


def local_kernel(
    count, heads, wide, both, queries_hbm, keys_hbm, values_hbm, local, queries, keys, values, sems
):
    def copies(b):
        rows = pl.ds(b * BLOCK, BLOCK)
        pairs = ((queries_hbm, queries), (keys_hbm, keys), (values_hbm, values))
        return [
            pltpu.make_async_copy(source.at[rows], target.at[rows], sems.at[i, b])
            for i, (source, target) in enumerate(pairs)
        ]

    for b in range(count):
        for copy in copies(b):
            copy.start()
    second = lax.axis_index("c") == 1
    inner = lax.broadcasted_iota(jnp.int32, (BLOCK, E), 0).astype(F32)
    row = lax.broadcasted_iota(jnp.int32, (BLOCK, BLOCK), 0)
    column = lax.broadcasted_iota(jnp.int32, (BLOCK, BLOCK), 1)
    distance = (row - column).astype(F32)
    for b in range(count):
        for copy in copies(b):
            copy.wait()
    for h in range(heads):
        rate = jnp.concatenate([wide[h, 0:1]] * (BLOCK // E), axis=1)
        masked = jnp.where(distance >= 0, power(rate, jnp.maximum(distance, 0.0)), 0.0)
        scale = power(wide[h, 0:1], inner + 1.0)
        key_scale = power(wide[h, 0:1], BLOCK - 1.0 - inner)
        held = jnp.where(second, both[0, h], 0.0)
        for b in range(count):
            rows = pl.ds(b * BLOCK, BLOCK)
            query = queries[rows, head_columns(h)]
            scores = lax.dot_general(
                query, keys[rows, head_columns(h)], (((1,), (1,)), ((), ())), preferred_element_type=F32
            )
            weights = (scores * masked).astype(BF16)
            out = jnp.dot(weights, values[rows, head_columns(h)], preferred_element_type=F32)
            doubled = jnp.concatenate([query, query], axis=1)
            carried = jnp.dot(doubled, two_halves(held), preferred_element_type=F32)
            local[rows, head_columns(h)] = out + carried * scale
            if b < count - 1:
                scaled = keys[rows, head_columns(h)].astype(F32) * key_scale
                block = lax.dot_general(
                    scaled.astype(BF16),
                    values[rows, head_columns(h)],
                    (((0,), (0,)), ((), ())),
                    preferred_element_type=F32,
                )
                held = held * power(wide[h, 0:1], float(BLOCK)) + block


def mix_kernel(count, heads, wide, queries, local, prefix, mixed, squares, scale):
    length = float(count * BLOCK)
    second = lax.axis_index("c") == 1
    inner = lax.broadcasted_iota(jnp.int32, (BLOCK, E), 0).astype(F32)
    entering = []
    for h in range(heads):
        scale[h] = power(wide[h, 0:1], inner + 1.0)
        entering.append(two_halves(prefix[h] * jnp.where(second, power(wide[h, 0:1], length), 1.0)))
    for b in range(count):
        rows = pl.ds(b * BLOCK, BLOCK)
        total = jnp.zeros((BLOCK, E), F32)
        for h in range(heads):
            query = queries[rows, head_columns(h)]
            doubled = jnp.concatenate([query, query], axis=1)
            out = jnp.dot(doubled, entering[h], preferred_element_type=F32)
            factor = scale[h] * power(wide[h, 0:1], float(b * BLOCK)) if b > 0 else scale[h]
            out = local[rows, head_columns(h)] + out * factor
            mixed[rows, head_columns(h)] = out
            total = total + out * out
        sums = lax.dot_general(
            jnp.ones((8, E), F32),
            total,
            (((1,), (1,)), ((), ())),
            precision=lax.Precision.HIGHEST,
            preferred_element_type=F32,
        )
        for r in range(BLOCK // E):
            row = jnp.broadcast_to(sums[0:1, r * E : (r + 1) * E], (squares.shape[0], E))
            squares[:, b * (BLOCK // E) + r, :] = row


def norm_kernel(count, mixed, squares, gain, out_hbm, out, sems):
    sums = squares[0]
    for i in range(1, squares.shape[0]):
        sums = sums + squares[i]
    inverse = lax.rsqrt(sums / float(H * E) + EPSILON)
    tiles = out.shape[0] // E
    for t in range(tiles):
        rows = pl.ds(t * E, E)
        column = jnp.broadcast_to(inverse[t : t + 1, :], (E, E)).T
        for h in range(out.shape[1] // E):
            part = mixed[rows, head_columns(h)] * column * gain[:, head_columns(h)]
            out[rows, head_columns(h)] = part.astype(BF16)
        if t % 2 == 1:
            pair = pl.ds((t - 1) * E, 2 * E)
            pltpu.make_async_copy(out.at[pair], out_hbm.at[pair], sems.at[t // 2]).start()
    for t in range(1, tiles, 2):
        pair = pl.ds((t - 1) * E, 2 * E)
        pltpu.make_async_copy(out.at[pair], out_hbm.at[pair], sems.at[t // 2]).wait()


def body(queries, key_rows, value_rows, decay_rates, out_gain):
    length, width = queries.shape
    heads = decay_rates.shape[0]
    count = length // BLOCK
    half = heads // 2
    chips = lax.axis_size("z") * lax.axis_size("x")
    parts = lax.axis_size(HEAD)
    shape = jax.ShapeDtypeStruct

    state, wide = call(
        functools.partial(states_kernel, count, heads),
        (
            shape((heads, E, E), F32),
            shape((heads, 8, E), F32),
        ),
        [HBM, HBM, HBM],
        (VMEM, VMEM),
        [
            pltpu.VMEM((length, width), BF16),
            pltpu.VMEM((length, width), BF16),
            pltpu.VMEM((heads, BLOCK, E), F32),
            pltpu.SMEM((heads,), F32),
            pltpu.SemaphoreType.DMA((2, count)),
            pltpu.SemaphoreType.DMA,
        ],
        room=STATES_ROOM,
        flops=2 * length * E * width,
        moved=4 * length * width,
        name="states",
    )(decay_rates, key_rows, value_rows)
    both = lax.all_gather(state, "c")
    total = call(
        functools.partial(chip_kernel, length, half),
        shape((half, E, E), F32),
        [VMEM, VMEM],
        VMEM,
        name="chip",
    )(wide, both)
    owned = lax.all_to_all(total.reshape(chips, -1, E), CHIPS, 0, 0, tiled=True)
    prefixes = call(
        functools.partial(scan_kernel, length, half, chips),
        shape(owned.shape, F32),
        [VMEM, VMEM],
        VMEM,
        name="scan",
    )(wide, owned)
    mine = lax.all_to_all(prefixes, CHIPS, 0, 0, tiled=True).reshape(half, E, E)
    prefix = lax.all_gather(mine, "c", tiled=True)
    local, staged = call(
        functools.partial(local_kernel, count, heads),
        (shape((length, width), F32), shape((length, width), BF16)),
        [VMEM, VMEM, HBM, HBM, HBM],
        (VMEM, VMEM),
        [
            pltpu.VMEM((length, width), BF16),
            pltpu.VMEM((length, width), BF16),
            pltpu.SemaphoreType.DMA((3, count)),
        ],
        room=LOCAL_ROOM,
        flops=1 << 40,
        moved=0,
        name="local",
    )(wide, both, queries, key_rows, value_rows)
    mixed, squares = call(
        functools.partial(mix_kernel, count, heads),
        (shape((length, width), F32), shape((parts, length // E, E), F32)),
        [VMEM] * 4,
        (VMEM, VMEM),
        [pltpu.VMEM((heads, BLOCK, E), F32)],
        flops=4 * length * E * width,
        moved=10 * length * width,
        name="mix",
    )(wide, staged, local, prefix)
    shared = lax.all_to_all(squares, HEAD, 0, 0, tiled=True)
    return call(
        functools.partial(norm_kernel, count),
        shape((length, width), BF16),
        [VMEM, VMEM, VMEM],
        HBM,
        [pltpu.VMEM((length, width), BF16), pltpu.SemaphoreType.DMA((count,))],
        moved=6 * length * width,
        name="norm",
    )(mixed, shared, out_gain.reshape(1, width))


def solution(mesh):
    torus = Mesh(mesh.devices.reshape(8, 4, 2, mesh.shape["head"]), ("z", "x", "c", "head"))
    in_specs = (P(SEQ, "head"), P(SEQ, "head"), P(SEQ, "head"), P("head"), P("head"))
    return jax.shard_map(
        body, mesh=torus, in_specs=in_specs, out_specs=P(SEQ, "head"), check_vma=False
    )
```

```python
import functools

import jax
import jax.numpy as jnp
from jax import lax
from jax.experimental import pallas as pl
from jax.experimental.pallas import tpu as pltpu
from jax.sharding import Mesh
from jax.sharding import PartitionSpec as P

H = 32
E = 128
BLOCK = 256
EPSILON = 1e-06
SEQ = ("z", "x", "c")
CHIPS = ("z", "x")
HEAD = "head"

F32 = jnp.float32
BF16 = jnp.bfloat16
VMEM_BYTES = 67043328
STATES_ROOM = 11 << 20
LOCAL_ROOM = 3 << 20
MIX_ROOM = 16 << 20
SPARE = 8
VMEM = pl.BlockSpec(memory_space=pltpu.VMEM)
HBM = pl.BlockSpec(memory_space=pltpu.HBM)


def call(kernel, outs, ins, out_specs, scratch=(), room=40 << 20, flops=0, moved=0, name=None):
    return pl.pallas_call(
        kernel,
        out_shape=outs,
        in_specs=ins,
        out_specs=out_specs,
        scratch_shapes=list(scratch),
        compiler_params=pltpu.CompilerParams(vmem_limit_bytes=VMEM_BYTES - room),
        cost_estimate=pl.CostEstimate(flops=flops, bytes_accessed=moved, transcendentals=0),
        name=name,
    )


def power(rate, distance):
    return jnp.exp(-rate * distance)


def head_columns(h):
    return slice(h * E, (h + 1) * E)


def states_kernel(
    count, heads, rates_hbm, keys_hbm, values_hbm, state, wide, keys, values, scale, rates, sems, rate_sem
):
    def copies(b):
        rows = pl.ds(b * BLOCK, BLOCK)
        return (
            pltpu.make_async_copy(keys_hbm.at[rows], keys.at[rows], sems.at[0, b]),
            pltpu.make_async_copy(values_hbm.at[rows], values.at[rows], sems.at[1, b]),
        )

    rate_copy = pltpu.make_async_copy(rates_hbm, rates, rate_sem)
    rate_copy.start()
    for b in range(count):
        for copy in copies(b):
            copy.start()
    inner = lax.broadcasted_iota(jnp.int32, (BLOCK, E), 0).astype(F32)
    rate_copy.wait()
    for h in range(heads):
        wide[h] = jnp.full((8, E), rates[h], F32)
        scale[h] = power(rates[h], BLOCK - 1.0 - inner)
    for b in range(count):
        rows = pl.ds(b * BLOCK, BLOCK)
        for copy in copies(b):
            copy.wait()
        for h in range(heads):
            scaled = keys[rows, head_columns(h)].astype(F32) * scale[h]
            block = lax.dot_general(
                scaled.astype(BF16),
                values[rows, head_columns(h)],
                (((0,), (0,)), ((), ())),
                preferred_element_type=F32,
            )
            if b > 0:
                block = state[h] * power(wide[h, 0:1], float(BLOCK)) + block
            state[h] = block


def chip_kernel(length, half, wide, both, total):
    first = lax.axis_index("c") * half
    for i in range(half):
        decay = power(wide[first + i, 0:1], float(length))
        total[i] = both[0, first + i] * decay + both[1, first + i]


def scan_kernel(length, half, chips, wide, totals, prefixes):
    piece = lax.axis_index("z") * lax.axis_size("x") + lax.axis_index("x")
    h = lax.axis_index("c") * half + piece // (chips // half)
    decay = power(wide[h], 2.0 * length)
    running = jnp.zeros(totals.shape[1:], F32)
    for i in range(chips):
        prefixes[i] = running
        running = running * decay + totals[i]


def two_halves(matrix):
    high = matrix.astype(BF16)
    low = (matrix - high.astype(F32)).astype(BF16)
    return jnp.concatenate([high, low], axis=0)


def decay_mask(rate):
    row = lax.broadcasted_iota(jnp.int32, (E, E), 0)
    column = lax.broadcasted_iota(jnp.int32, (E, E), 1)
    distance = (row - column).astype(F32)
    within = jnp.where(distance >= 0, power(rate, jnp.maximum(distance, 0.0)), 0.0)
    to_row = power(rate, row.astype(F32))
    across = to_row * power(rate, (E - column[0:1]).astype(F32))
    return within, across


def local_kernel(
    count, heads, wide, both, queries_hbm, keys_hbm, values_hbm, local_hbm, staged_hbm,
    local, queries, keys, values, held, scale, key_scale, within, across, rates, sems, out_sems, rate_sem,
):
    def copies(b):
        rows = pl.ds(b * BLOCK, BLOCK)
        pairs = ((keys_hbm, keys), (queries_hbm, queries), (values_hbm, values))
        return [
            pltpu.make_async_copy(source.at[rows], target.at[rows], sems.at[i, b])
            for i, (source, target) in enumerate(pairs)
        ]

    def stores(b):
        rows = pl.ds(b * BLOCK, BLOCK)
        return [
            pltpu.make_async_copy(local.at[rows], local_hbm.at[rows], out_sems.at[0, b]),
            pltpu.make_async_copy(queries.at[rows], staged_hbm.at[rows], out_sems.at[1, b]),
        ]

    for b in range(count):
        for copy in copies(b):
            copy.start()
    second = lax.axis_index("c") == 1
    inner = lax.broadcasted_iota(jnp.int32, (BLOCK, E), 0).astype(F32)
    for h in range(heads):
        rates[:, head_columns(h)] = wide[h]
    rate_copy = pltpu.make_async_copy(rates, local_hbm.at[pl.ds(count * BLOCK, 8)], rate_sem)
    rate_copy.start()
    for h in range(heads):
        rate = wide[h, 0:1]
        within[h], across[h] = decay_mask(rate)
        scale[h] = power(rate, inner + 1.0)
        key_scale[h] = power(rate, BLOCK - 1.0 - inner)
        held[h] = jnp.where(second, both[0, h], 0.0)
    top, bottom = slice(0, E), slice(E, BLOCK)
    for b in range(count):
        rows = pl.ds(b * BLOCK, BLOCK)
        for copy in copies(b):
            copy.wait()
        for h in range(heads):
            query = queries[rows, head_columns(h)]
            key = keys[rows, head_columns(h)]
            value = values[rows, head_columns(h)]
            scores = lax.dot_general(
                query, key, (((1,), (1,)), ((), ())), preferred_element_type=F32
            )
            upper = (scores[top, top] * within[h]).astype(BF16)
            left = (scores[bottom, top] * across[h]).astype(BF16)
            right = (scores[bottom, bottom] * within[h]).astype(BF16)
            weights = jnp.concatenate(
                [
                    jnp.concatenate([upper, jnp.zeros((E, E), BF16)], axis=1),
                    jnp.concatenate([left, right], axis=1),
                ],
                axis=0,
            )
            out = jnp.dot(weights, value, preferred_element_type=F32)
            doubled = jnp.concatenate([query, query], axis=1)
            carried = jnp.dot(doubled, two_halves(held[h]), preferred_element_type=F32)
            local[rows, head_columns(h)] = out + carried * scale[h]
            if b < count - 1:
                scaled = (key.astype(F32) * key_scale[h]).astype(BF16)
                block = lax.dot_general(
                    scaled, value, (((0,), (0,)), ((), ())), preferred_element_type=F32
                )
                held[h] = held[h] * power(wide[h, 0:1], float(BLOCK)) + block
        for copy in stores(b):
            copy.start()
    for b in range(count):
        for copy in stores(b):
            copy.wait()
    rate_copy.wait()


def mix_kernel(
    count, heads, queries_hbm, local_hbm, prefix, mixed, squares, scale, queries, local, rates, sems, rate_sem
):
    def copies(b):
        rows = pl.ds(b * BLOCK, BLOCK)
        return (
            pltpu.make_async_copy(queries_hbm.at[rows], queries.at[rows], sems.at[0, b]),
            pltpu.make_async_copy(local_hbm.at[rows], local.at[rows], sems.at[1, b]),
        )

    rate_copy = pltpu.make_async_copy(local_hbm.at[pl.ds(count * BLOCK, 8)], rates, rate_sem)
    rate_copy.start()
    for b in range(count):
        for copy in copies(b):
            copy.start()
    length = float(count * BLOCK)
    second = lax.axis_index("c") == 1
    inner = lax.broadcasted_iota(jnp.int32, (BLOCK, E), 0).astype(F32)
    rate_copy.wait()
    entering = []
    for h in range(heads):
        rate = rates[0:1, head_columns(h)]
        scale[h] = power(rate, inner + 1.0)
        entering.append(two_halves(prefix[h] * jnp.where(second, power(rate, length), 1.0)))
    for b in range(count):
        rows = pl.ds(b * BLOCK, BLOCK)
        for copy in copies(b):
            copy.wait()
        total = jnp.zeros((BLOCK, E), F32)
        for h in range(heads):
            query = queries[rows, head_columns(h)]
            doubled = jnp.concatenate([query, query], axis=1)
            out = jnp.dot(doubled, entering[h], preferred_element_type=F32)
            decay = power(rates[0:1, head_columns(h)], float(b * BLOCK))
            factor = scale[h] * decay if b > 0 else scale[h]
            out = local[rows, head_columns(h)] + out * factor
            mixed[rows, head_columns(h)] = out
            total = total + out * out
        sums = lax.dot_general(
            jnp.ones((8, E), F32),
            total,
            (((1,), (1,)), ((), ())),
            precision=lax.Precision.HIGHEST,
            preferred_element_type=F32,
        )
        for r in range(BLOCK // E):
            row = jnp.broadcast_to(sums[0:1, r * E : (r + 1) * E], (squares.shape[0], E))
            squares[:, b * (BLOCK // E) + r, :] = row


def norm_kernel(count, mixed, squares, gain, out_hbm, out, sems):
    sums = squares[0]
    for i in range(1, squares.shape[0]):
        sums = sums + squares[i]
    inverse = lax.rsqrt(sums / float(H * E) + EPSILON)
    tiles = out.shape[0] // E
    for t in range(tiles):
        rows = pl.ds(t * E, E)
        column = jnp.broadcast_to(inverse[t : t + 1, :], (E, E)).T
        for h in range(out.shape[1] // E):
            part = mixed[rows, head_columns(h)] * column * gain[:, head_columns(h)]
            out[rows, head_columns(h)] = part.astype(BF16)
        if t % 2 == 1:
            pair = pl.ds((t - 1) * E, 2 * E)
            pltpu.make_async_copy(out.at[pair], out_hbm.at[pair], sems.at[t // 2]).start()
    for t in range(1, tiles, 2):
        pair = pl.ds((t - 1) * E, 2 * E)
        pltpu.make_async_copy(out.at[pair], out_hbm.at[pair], sems.at[t // 2]).wait()


def body(queries, key_rows, value_rows, decay_rates, out_gain):
    length, width = queries.shape
    heads = decay_rates.shape[0]
    count = length // BLOCK
    half = heads // 2
    chips = lax.axis_size("z") * lax.axis_size("x")
    parts = lax.axis_size(HEAD)
    shape = jax.ShapeDtypeStruct

    state, wide = call(
        functools.partial(states_kernel, count, heads),
        (
            shape((heads, E, E), F32),
            shape((heads, 8, E), F32),
        ),
        [HBM, HBM, HBM],
        (VMEM, VMEM),
        [
            pltpu.VMEM((length, width), BF16),
            pltpu.VMEM((length, width), BF16),
            pltpu.VMEM((heads, BLOCK, E), F32),
            pltpu.SMEM((heads,), F32),
            pltpu.SemaphoreType.DMA((2, count)),
            pltpu.SemaphoreType.DMA,
        ],
        room=STATES_ROOM,
        flops=2 * length * E * width,
        moved=4 * length * width,
        name="states",
    )(decay_rates, key_rows, value_rows)
    both = lax.all_gather(state, "c")
    total = call(
        functools.partial(chip_kernel, length, half),
        shape((half, E, E), F32),
        [VMEM, VMEM],
        VMEM,
        name="chip",
    )(wide, both)
    owned = lax.all_to_all(total.reshape(chips, -1, E), CHIPS, 0, 0, tiled=True)
    prefixes = call(
        functools.partial(scan_kernel, length, half, chips),
        shape(owned.shape, F32),
        [VMEM, VMEM],
        VMEM,
        name="scan",
    )(wide, owned)
    mine = lax.all_to_all(prefixes, CHIPS, 0, 0, tiled=True).reshape(half, E, E)
    prefix = lax.all_gather(mine, "c", tiled=True)
    local, staged = call(
        functools.partial(local_kernel, count, heads),
        (shape((SPARE * length, width), F32), shape((SPARE * length, width), BF16)),
        [VMEM, VMEM, HBM, HBM, HBM],
        (HBM, HBM),
        [
            pltpu.VMEM((length, width), F32),
            pltpu.VMEM((length, width), BF16),
            pltpu.VMEM((length, width), BF16),
            pltpu.VMEM((length, width), BF16),
            pltpu.VMEM((heads, E, E), F32),
            pltpu.VMEM((heads, BLOCK, E), F32),
            pltpu.VMEM((heads, BLOCK, E), F32),
            pltpu.VMEM((heads, E, E), F32),
            pltpu.VMEM((heads, E, E), F32),
            pltpu.VMEM((8, width), F32),
            pltpu.SemaphoreType.DMA((3, count)),
            pltpu.SemaphoreType.DMA((2, count)),
            pltpu.SemaphoreType.DMA,
        ],
        room=LOCAL_ROOM,
        flops=8 * length * BLOCK * width,
        moved=12 * length * width,
        name="local",
    )(wide, both, queries, key_rows, value_rows)
    mixed, squares = call(
        functools.partial(mix_kernel, count, heads),
        (shape((length, width), F32), shape((parts, length // E, E), F32)),
        [HBM, HBM, VMEM],
        (VMEM, VMEM),
        [
            pltpu.VMEM((heads, BLOCK, E), F32),
            pltpu.VMEM((length, width), BF16),
            pltpu.VMEM((length, width), F32),
            pltpu.VMEM((8, width), F32),
            pltpu.SemaphoreType.DMA((2, count)),
            pltpu.SemaphoreType.DMA,
        ],
        room=MIX_ROOM,
        flops=4 * length * E * width,
        moved=10 * length * width,
        name="mix",
    )(staged, local, prefix)
    shared = lax.all_to_all(squares, HEAD, 0, 0, tiled=True)
    return call(
        functools.partial(norm_kernel, count),
        shape((length, width), BF16),
        [VMEM, VMEM, VMEM],
        HBM,
        [pltpu.VMEM((length, width), BF16), pltpu.SemaphoreType.DMA((count,))],
        moved=6 * length * width,
        name="norm",
    )(mixed, shared, out_gain.reshape(1, width))


def solution(mesh):
    torus = Mesh(mesh.devices.reshape(8, 4, 2, mesh.shape["head"]), ("z", "x", "c", "head"))
    in_specs = (P(SEQ, "head"), P(SEQ, "head"), P(SEQ, "head"), P("head"), P("head"))
    return jax.shard_map(
        body, mesh=torus, in_specs=in_specs, out_specs=P(SEQ, "head"), check_vma=False
    )
```

```python
import functools

import jax
import jax.numpy as jnp
from jax import lax
from jax.experimental import pallas as pl
from jax.experimental.pallas import tpu as pltpu
from jax.sharding import Mesh
from jax.sharding import PartitionSpec as P

H = 32
E = 128
BLOCK = 256
EPSILON = 1e-06
SEQ = ("z", "x", "c")
CHIPS = ("z", "x")
HEAD = "head"

F32 = jnp.float32
BF16 = jnp.bfloat16
VMEM_BYTES = 67043328
STATES_ROOM = 11 << 20
LOCAL_ROOM = 40 << 20
ROWS = 128
DECAY_FLOPS = 1 << 30
DECAY_MOVED = 8 << 20
VMEM = pl.BlockSpec(memory_space=pltpu.VMEM)
HBM = pl.BlockSpec(memory_space=pltpu.HBM)


def call(kernel, outs, ins, out_specs, scratch=(), room=40 << 20, flops=0, moved=0, name=None):
    return pl.pallas_call(
        kernel,
        out_shape=outs,
        in_specs=ins,
        out_specs=out_specs,
        scratch_shapes=list(scratch),
        compiler_params=pltpu.CompilerParams(vmem_limit_bytes=VMEM_BYTES - room),
        cost_estimate=pl.CostEstimate(flops=flops, bytes_accessed=moved, transcendentals=0),
        name=name,
    )


def power(rate, distance):
    return jnp.exp(-rate * distance)


def head_columns(h):
    return slice(h * E, (h + 1) * E)


def states_kernel(
    count, heads, rates_hbm, keys_hbm, values_hbm, state, wide, keys, values, scale, rates, sems, rate_sem
):
    def copies(b):
        rows = pl.ds(b * BLOCK, BLOCK)
        return (
            pltpu.make_async_copy(keys_hbm.at[rows], keys.at[rows], sems.at[0, b]),
            pltpu.make_async_copy(values_hbm.at[rows], values.at[rows], sems.at[1, b]),
        )

    rate_copy = pltpu.make_async_copy(rates_hbm, rates, rate_sem)
    rate_copy.start()
    for b in range(count):
        for copy in copies(b):
            copy.start()
    inner = lax.broadcasted_iota(jnp.int32, (BLOCK, E), 0).astype(F32)
    rate_copy.wait()
    for h in range(heads):
        wide[h] = jnp.full((8, E), rates[h], F32)
        scale[h] = power(rates[h], BLOCK - 1.0 - inner)
    for b in range(count):
        rows = pl.ds(b * BLOCK, BLOCK)
        for copy in copies(b):
            copy.wait()
        for h in range(heads):
            scaled = keys[rows, head_columns(h)].astype(F32) * scale[h]
            block = lax.dot_general(
                scaled.astype(BF16),
                values[rows, head_columns(h)],
                (((0,), (0,)), ((), ())),
                preferred_element_type=F32,
            )
            if b > 0:
                block = state[h] * power(wide[h, 0:1], float(BLOCK)) + block
            state[h] = block


def chip_kernel(length, half, wide, both, total):
    first = lax.axis_index("c") * half
    for i in range(half):
        decay = power(wide[first + i, 0:1], float(length))
        total[i] = both[0, first + i] * decay + both[1, first + i]


def scan_kernel(length, half, chips, wide, totals, prefixes):
    piece = lax.axis_index("z") * lax.axis_size("x") + lax.axis_index("x")
    h = lax.axis_index("c") * half + piece // (chips // half)
    decay = power(wide[h], 2.0 * length)
    running = jnp.zeros(totals.shape[1:], F32)
    for i in range(chips):
        prefixes[i] = running
        running = running * decay + totals[i]


def two_halves(matrix):
    high = matrix.astype(BF16)
    low = (matrix - high.astype(F32)).astype(BF16)
    return jnp.concatenate([high, low], axis=0)


def decay_mask(rate):
    row = lax.broadcasted_iota(jnp.int32, (E, E), 0)
    column = lax.broadcasted_iota(jnp.int32, (E, E), 1)
    distance = (row - column).astype(F32)
    within = jnp.where(distance >= 0, power(rate, jnp.maximum(distance, 0.0)), 0.0)
    to_row = power(rate, row.astype(F32))
    across = to_row * power(rate, (E - column[0:1]).astype(F32))
    return within, across


def decay_kernel(heads, wide, within, across, scale, key_scale):
    inner = lax.broadcasted_iota(jnp.int32, (BLOCK, E), 0).astype(F32)
    for h in range(heads):
        rate = wide[h, 0:1]
        within[h], across[h] = decay_mask(rate)
        scale[h] = power(rate, inner + 1.0)
        key_scale[h] = power(rate, BLOCK - 1.0 - inner)


def local_kernel(
    count, heads, wide, within, across, scale, key_scale, both, queries, keys, values, local, held
):
    second = lax.axis_index("c") == 1
    for h in range(heads):
        held[h] = jnp.where(second, both[0, h], 0.0)
    top, bottom = slice(0, E), slice(E, BLOCK)
    for b in range(count):
        rows = pl.ds(b * BLOCK, BLOCK)
        for h in range(heads):
            query = queries[rows, head_columns(h)]
            key = keys[rows, head_columns(h)]
            value = values[rows, head_columns(h)]
            scores = lax.dot_general(
                query, key, (((1,), (1,)), ((), ())), preferred_element_type=F32
            )
            upper = (scores[top, top] * within[h]).astype(BF16)
            left = (scores[bottom, top] * across[h]).astype(BF16)
            right = (scores[bottom, bottom] * within[h]).astype(BF16)
            weights = jnp.concatenate(
                [
                    jnp.concatenate([upper, jnp.zeros((E, E), BF16)], axis=1),
                    jnp.concatenate([left, right], axis=1),
                ],
                axis=0,
            )
            out = jnp.dot(weights, value, preferred_element_type=F32)
            doubled = jnp.concatenate([query, query], axis=1)
            carried = jnp.dot(doubled, two_halves(held[h]), preferred_element_type=F32)
            local[rows, head_columns(h)] = out + carried * scale[h]
            if b < count - 1:
                scaled = (key.astype(F32) * key_scale[h]).astype(BF16)
                block = lax.dot_general(
                    scaled, value, (((0,), (0,)), ((), ())), preferred_element_type=F32
                )
                held[h] = held[h] * power(wide[h, 0:1], float(BLOCK)) + block


def relay_kernel(mine, prefix):
    prefix[...] = mine[...]


def mix_kernel(count, heads, wide, scale, queries, local, prefix, mixed, squares):
    length = float(count * BLOCK)
    second = lax.axis_index("c") == 1
    entering = []
    for h in range(heads):
        entering.append(two_halves(prefix[h] * jnp.where(second, power(wide[h, 0:1], length), 1.0)))
    for t in range(count * BLOCK // ROWS):
        rows = pl.ds(t * ROWS, ROWS)
        inner = t * ROWS % BLOCK
        block = t * ROWS // BLOCK
        total = jnp.zeros((ROWS, E), F32)
        for h in range(heads):
            query = queries[rows, head_columns(h)]
            doubled = jnp.concatenate([query, query], axis=1)
            out = jnp.dot(doubled, entering[h], preferred_element_type=F32)
            factor = scale[h, inner : inner + ROWS]
            if block > 0:
                factor = factor * power(wide[h, 0:1], float(block * BLOCK))
            out = local[rows, head_columns(h)] + out * factor
            mixed[rows, head_columns(h)] = out
            total = total + out * out
        for r in range(ROWS // E):
            sums = jnp.sum(total[r * E : (r + 1) * E].T, axis=0, keepdims=True)
            squares[:, t * (ROWS // E) + r, :] = jnp.broadcast_to(sums, (squares.shape[0], E))


def norm_kernel(count, mixed, squares, gain, out_hbm, out, sems):
    sums = squares[0]
    for i in range(1, squares.shape[0]):
        sums = sums + squares[i]
    inverse = lax.rsqrt(sums / float(H * E) + EPSILON)
    tiles = out.shape[0] // E
    for t in range(tiles):
        rows = pl.ds(t * E, E)
        column = jnp.broadcast_to(inverse[t : t + 1, :], (E, E)).T
        for h in range(out.shape[1] // E):
            part = mixed[rows, head_columns(h)] * column * gain[:, head_columns(h)]
            out[rows, head_columns(h)] = part.astype(BF16)
        if t % 2 == 1:
            pair = pl.ds((t - 1) * E, 2 * E)
            pltpu.make_async_copy(out.at[pair], out_hbm.at[pair], sems.at[t // 2]).start()
    for t in range(1, tiles, 2):
        pair = pl.ds((t - 1) * E, 2 * E)
        pltpu.make_async_copy(out.at[pair], out_hbm.at[pair], sems.at[t // 2]).wait()


def body(queries, key_rows, value_rows, decay_rates, out_gain):
    length, width = queries.shape
    heads = decay_rates.shape[0]
    count = length // BLOCK
    half = heads // 2
    chips = lax.axis_size("z") * lax.axis_size("x")
    parts = lax.axis_size(HEAD)
    shape = jax.ShapeDtypeStruct

    state, wide = call(
        functools.partial(states_kernel, count, heads),
        (
            shape((heads, E, E), F32),
            shape((heads, 8, E), F32),
        ),
        [HBM, HBM, HBM],
        (VMEM, VMEM),
        [
            pltpu.VMEM((length, width), BF16),
            pltpu.VMEM((length, width), BF16),
            pltpu.VMEM((heads, BLOCK, E), F32),
            pltpu.SMEM((heads,), F32),
            pltpu.SemaphoreType.DMA((2, count)),
            pltpu.SemaphoreType.DMA,
        ],
        room=STATES_ROOM,
        flops=2 * length * E * width,
        moved=4 * length * width,
        name="states",
    )(decay_rates, key_rows, value_rows)
    both = lax.all_gather(state, "c")
    total = call(
        functools.partial(chip_kernel, length, half),
        shape((half, E, E), F32),
        [VMEM, VMEM],
        VMEM,
        name="chip",
    )(wide, both)
    owned = lax.all_to_all(total.reshape(chips, -1, E), CHIPS, 0, 0, tiled=True)
    prefixes = call(
        functools.partial(scan_kernel, length, half, chips),
        shape(owned.shape, F32),
        [VMEM, VMEM],
        VMEM,
        name="scan",
    )(wide, owned)
    mine = lax.all_to_all(prefixes, CHIPS, 0, 0, tiled=True).reshape(half, E, E)
    mine = call(
        relay_kernel,
        shape(mine.shape, F32),
        [VMEM],
        VMEM,
        flops=DECAY_FLOPS,
        moved=DECAY_MOVED,
        name="relay",
    )(mine)
    prefix = lax.all_gather(mine, "c", tiled=True)
    decays = call(
        functools.partial(decay_kernel, heads),
        (
            shape((heads, E, E), F32),
            shape((heads, E, E), F32),
            shape((heads, BLOCK, E), F32),
            shape((heads, BLOCK, E), F32),
        ),
        [VMEM],
        (VMEM,) * 4,
        flops=DECAY_FLOPS,
        moved=DECAY_MOVED,
        name="decays",
    )(wide)
    local = call(
        functools.partial(local_kernel, count, heads),
        shape((length, width), F32),
        [VMEM] * 9,
        VMEM,
        [pltpu.VMEM((heads, E, E), F32)],
        room=LOCAL_ROOM,
        flops=8 * length * BLOCK * width,
        moved=10 * length * width,
        name="local",
    )(wide, *decays, both, queries, key_rows, value_rows)
    mixed, squares = call(
        functools.partial(mix_kernel, count, heads),
        (shape((length, width), F32), shape((parts, length // E, E), F32)),
        [VMEM] * 5,
        (VMEM, VMEM),
        flops=4 * length * E * width,
        moved=10 * length * width,
        name="mix",
    )(wide, decays[2], queries, local, prefix)
    shared = lax.all_to_all(squares, HEAD, 0, 0, tiled=True)
    return call(
        functools.partial(norm_kernel, count),
        shape((length, width), BF16),
        [VMEM, VMEM, VMEM],
        HBM,
        [pltpu.VMEM((length, width), BF16), pltpu.SemaphoreType.DMA((count,))],
        moved=6 * length * width,
        name="norm",
    )(mixed, shared, out_gain.reshape(1, width))


def solution(mesh):
    torus = Mesh(mesh.devices.reshape(8, 4, 2, mesh.shape["head"]), ("z", "x", "c", "head"))
    in_specs = (P(SEQ, "head"), P(SEQ, "head"), P(SEQ, "head"), P("head"), P("head"))
    return jax.shard_map(
        body, mesh=torus, in_specs=in_specs, out_specs=P(SEQ, "head"), check_vma=False
    )
```

```python
import functools

import jax
import jax.numpy as jnp
from jax import lax
from jax.experimental import pallas as pl
from jax.experimental.pallas import tpu as pltpu
from jax.sharding import Mesh
from jax.sharding import PartitionSpec as P

H = 32
E = 128
BLOCK = 256
EPSILON = 1e-06
SEQ = ("z", "x", "c")
CHIPS = ("z", "x")
HEAD = "head"

F32 = jnp.float32
BF16 = jnp.bfloat16
VMEM_BYTES = 67043328
LOCAL_ROOM = 40 << 20
ROWS = 128
DECAY_FLOPS = 1 << 30
DECAY_MOVED = 8 << 20
VMEM = pl.BlockSpec(memory_space=pltpu.VMEM)
HBM = pl.BlockSpec(memory_space=pltpu.HBM)


def call(kernel, outs, ins, out_specs, scratch=(), room=40 << 20, flops=0, moved=0, name=None):
    return pl.pallas_call(
        kernel,
        out_shape=outs,
        in_specs=ins,
        out_specs=out_specs,
        scratch_shapes=list(scratch),
        compiler_params=pltpu.CompilerParams(vmem_limit_bytes=VMEM_BYTES - room),
        cost_estimate=pl.CostEstimate(flops=flops, bytes_accessed=moved, transcendentals=0),
        name=name,
    )


def power(rate, distance):
    return jnp.exp(-rate * distance)


def head_columns(h):
    return slice(h * E, (h + 1) * E)


def positions_kernel(inner):
    inner[...] = lax.broadcasted_iota(jnp.int32, inner.shape, 0).astype(F32)


def states_kernel(count, heads, inner, rates, keys, values, state, wide):
    for h in range(heads):
        rate = jnp.broadcast_to(rates[0:1, h : h + 1], (8, E))
        wide[h] = rate
        scale = power(rate[0:1], BLOCK - 1.0 - inner[...])
        decay = power(rate[0:1], float(BLOCK))
        total = None
        for b in range(count):
            rows = pl.ds(b * BLOCK, BLOCK)
            scaled = keys[rows, head_columns(h)].astype(F32) * scale
            block = lax.dot_general(
                scaled.astype(BF16),
                values[rows, head_columns(h)],
                (((0,), (0,)), ((), ())),
                preferred_element_type=F32,
            )
            total = block if b == 0 else total * decay + block
        state[h] = total


def chip_kernel(length, half, wide, both, total):
    first = lax.axis_index("c") * half
    for i in range(half):
        decay = power(wide[first + i, 0:1], float(length))
        total[i] = both[0, first + i] * decay + both[1, first + i]


def scan_kernel(length, half, chips, wide, totals, prefixes):
    piece = lax.axis_index("z") * lax.axis_size("x") + lax.axis_index("x")
    h = lax.axis_index("c") * half + piece // (chips // half)
    decay = power(wide[h], 2.0 * length)
    running = jnp.zeros(totals.shape[1:], F32)
    for i in range(chips):
        prefixes[i] = running
        running = running * decay + totals[i]


def two_halves(matrix):
    high = matrix.astype(BF16)
    low = (matrix - high.astype(F32)).astype(BF16)
    return jnp.concatenate([high, low], axis=0)


def decay_mask(rate):
    row = lax.broadcasted_iota(jnp.int32, (E, E), 0)
    column = lax.broadcasted_iota(jnp.int32, (E, E), 1)
    distance = (row - column).astype(F32)
    within = jnp.where(distance >= 0, power(rate, jnp.maximum(distance, 0.0)), 0.0)
    to_row = power(rate, row.astype(F32))
    across = to_row * power(rate, (E - column[0:1]).astype(F32))
    return within, across


def decay_kernel(heads, wide, within, across, scale, key_scale):
    inner = lax.broadcasted_iota(jnp.int32, (BLOCK, E), 0).astype(F32)
    for h in range(heads):
        rate = wide[h, 0:1]
        within[h], across[h] = decay_mask(rate)
        scale[h] = power(rate, inner + 1.0)
        key_scale[h] = power(rate, BLOCK - 1.0 - inner)


def local_kernel(
    count, heads, wide, within, across, scale, key_scale, both, queries, keys, values, local, held
):
    second = lax.axis_index("c") == 1
    for h in range(heads):
        held[h] = jnp.where(second, both[0, h], 0.0)
    top, bottom = slice(0, E), slice(E, BLOCK)
    for b in range(count):
        rows = pl.ds(b * BLOCK, BLOCK)
        for h in range(heads):
            query = queries[rows, head_columns(h)]
            key = keys[rows, head_columns(h)]
            value = values[rows, head_columns(h)]
            scores = lax.dot_general(
                query, key, (((1,), (1,)), ((), ())), preferred_element_type=F32
            )
            upper = (scores[top, top] * within[h]).astype(BF16)
            left = (scores[bottom, top] * across[h]).astype(BF16)
            right = (scores[bottom, bottom] * within[h]).astype(BF16)
            weights = jnp.concatenate(
                [
                    jnp.concatenate([upper, jnp.zeros((E, E), BF16)], axis=1),
                    jnp.concatenate([left, right], axis=1),
                ],
                axis=0,
            )
            out = jnp.dot(weights, value, preferred_element_type=F32)
            doubled = jnp.concatenate([query, query], axis=1)
            carried = jnp.dot(doubled, two_halves(held[h]), preferred_element_type=F32)
            local[rows, head_columns(h)] = out + carried * scale[h]
            if b < count - 1:
                scaled = (key.astype(F32) * key_scale[h]).astype(BF16)
                block = lax.dot_general(
                    scaled, value, (((0,), (0,)), ((), ())), preferred_element_type=F32
                )
                held[h] = held[h] * power(wide[h, 0:1], float(BLOCK)) + block


def relay_kernel(mine, prefix):
    prefix[...] = mine[...]


def mix_kernel(count, heads, wide, scale, queries, local, prefix, mixed, squares):
    length = float(count * BLOCK)
    second = lax.axis_index("c") == 1
    entering = []
    for h in range(heads):
        entering.append(two_halves(prefix[h] * jnp.where(second, power(wide[h, 0:1], length), 1.0)))
    for t in range(count * BLOCK // ROWS):
        rows = pl.ds(t * ROWS, ROWS)
        inner = t * ROWS % BLOCK
        block = t * ROWS // BLOCK
        total = jnp.zeros((ROWS, E), F32)
        for h in range(heads):
            query = queries[rows, head_columns(h)]
            doubled = jnp.concatenate([query, query], axis=1)
            out = jnp.dot(doubled, entering[h], preferred_element_type=F32)
            factor = scale[h, inner : inner + ROWS]
            if block > 0:
                factor = factor * power(wide[h, 0:1], float(block * BLOCK))
            out = local[rows, head_columns(h)] + out * factor
            mixed[rows, head_columns(h)] = out
            total = total + out * out
        for r in range(ROWS // E):
            sums = jnp.sum(total[r * E : (r + 1) * E].T, axis=0, keepdims=True)
            squares[:, t * (ROWS // E) + r, :] = jnp.broadcast_to(sums, (squares.shape[0], E))


def norm_kernel(count, mixed, squares, gain, out_hbm, out, sems):
    sums = squares[0]
    for i in range(1, squares.shape[0]):
        sums = sums + squares[i]
    inverse = lax.rsqrt(sums / float(H * E) + EPSILON)
    tiles = out.shape[0] // E
    for t in range(tiles):
        rows = pl.ds(t * E, E)
        column = jnp.broadcast_to(inverse[t : t + 1, :], (E, E)).T
        for h in range(out.shape[1] // E):
            part = mixed[rows, head_columns(h)] * column * gain[:, head_columns(h)]
            out[rows, head_columns(h)] = part.astype(BF16)
        pltpu.make_async_copy(out.at[rows], out_hbm.at[rows], sems.at[t]).start()
    for t in range(tiles):
        rows = pl.ds(t * E, E)
        pltpu.make_async_copy(out.at[rows], out_hbm.at[rows], sems.at[t]).wait()


def body(queries, key_rows, value_rows, decay_rates, out_gain):
    length, width = queries.shape
    heads = decay_rates.shape[0]
    count = length // BLOCK
    half = heads // 2
    chips = lax.axis_size("z") * lax.axis_size("x")
    parts = lax.axis_size(HEAD)
    shape = jax.ShapeDtypeStruct

    inner = call(
        positions_kernel,
        shape((BLOCK, E), F32),
        [],
        VMEM,
        flops=DECAY_FLOPS,
        moved=DECAY_MOVED,
        name="positions",
    )()
    state, wide = call(
        functools.partial(states_kernel, count, heads),
        (shape((heads, E, E), F32), shape((heads, 8, E), F32)),
        [VMEM] * 4,
        (VMEM, VMEM),
        flops=2 * length * E * width,
        moved=4 * length * width,
        name="states",
    )(inner, decay_rates.reshape(1, heads), key_rows, value_rows)
    both = lax.all_gather(state, "c")
    total = call(
        functools.partial(chip_kernel, length, half),
        shape((half, E, E), F32),
        [VMEM, VMEM],
        VMEM,
        name="chip",
    )(wide, both)
    owned = lax.all_to_all(total.reshape(chips, -1, E), CHIPS, 0, 0, tiled=True)
    prefixes = call(
        functools.partial(scan_kernel, length, half, chips),
        shape(owned.shape, F32),
        [VMEM, VMEM],
        VMEM,
        name="scan",
    )(wide, owned)
    mine = lax.all_to_all(prefixes, CHIPS, 0, 0, tiled=True).reshape(half, E, E)
    mine = call(
        relay_kernel,
        shape(mine.shape, F32),
        [VMEM],
        VMEM,
        flops=DECAY_FLOPS,
        moved=DECAY_MOVED,
        name="relay",
    )(mine)
    prefix = lax.all_gather(mine, "c", tiled=True)
    decays = call(
        functools.partial(decay_kernel, heads),
        (
            shape((heads, E, E), F32),
            shape((heads, E, E), F32),
            shape((heads, BLOCK, E), F32),
            shape((heads, BLOCK, E), F32),
        ),
        [VMEM],
        (VMEM,) * 4,
        flops=DECAY_FLOPS,
        moved=DECAY_MOVED,
        name="decays",
    )(wide)
    local = call(
        functools.partial(local_kernel, count, heads),
        shape((length, width), F32),
        [VMEM] * 9,
        VMEM,
        [pltpu.VMEM((heads, E, E), F32)],
        room=LOCAL_ROOM,
        flops=8 * length * BLOCK * width,
        moved=10 * length * width,
        name="local",
    )(wide, *decays, both, queries, key_rows, value_rows)
    mixed, squares = call(
        functools.partial(mix_kernel, count, heads),
        (shape((length, width), F32), shape((parts, length // E, E), F32)),
        [VMEM] * 5,
        (VMEM, VMEM),
        flops=4 * length * E * width,
        moved=10 * length * width,
        name="mix",
    )(wide, decays[2], queries, local, prefix)
    shared = lax.all_to_all(squares, HEAD, 0, 0, tiled=True)
    return call(
        functools.partial(norm_kernel, count),
        shape((length, width), BF16),
        [VMEM, VMEM, VMEM],
        HBM,
        [pltpu.VMEM((length, width), BF16), pltpu.SemaphoreType.DMA((length // E,))],
        moved=6 * length * width,
        name="norm",
    )(mixed, shared, out_gain.reshape(1, width))


def solution(mesh):
    torus = Mesh(mesh.devices.reshape(8, 4, 2, mesh.shape["head"]), ("z", "x", "c", "head"))
    in_specs = (P(SEQ, "head"), P(SEQ, "head"), P(SEQ, "head"), P("head"), P("head"))
    return jax.shard_map(
        body, mesh=torus, in_specs=in_specs, out_specs=P(SEQ, "head"), check_vma=False
    )
```

```python
import functools

import jax
import jax.numpy as jnp
from jax import lax
from jax.experimental import pallas as pl
from jax.experimental.pallas import tpu as pltpu
from jax.sharding import Mesh
from jax.sharding import PartitionSpec as P

H = 32
E = 128
BLOCK = 256
EPSILON = 1e-06
SEQ = ("z", "x", "c")
CHIPS = ("z", "x")
HEAD = "head"

F32 = jnp.float32
BF16 = jnp.bfloat16
VMEM_BYTES = 67043328
LOCAL_ROOM = 40 << 20
ROWS = 128
DECAY_FLOPS = 1 << 30
DECAY_MOVED = 8 << 20
VMEM = pl.BlockSpec(memory_space=pltpu.VMEM)
HBM = pl.BlockSpec(memory_space=pltpu.HBM)


def call(kernel, outs, ins, out_specs, scratch=(), room=40 << 20, flops=0, moved=0, name=None):
    return pl.pallas_call(
        kernel,
        out_shape=outs,
        in_specs=ins,
        out_specs=out_specs,
        scratch_shapes=list(scratch),
        compiler_params=pltpu.CompilerParams(vmem_limit_bytes=VMEM_BYTES - room),
        cost_estimate=pl.CostEstimate(flops=flops, bytes_accessed=moved, transcendentals=0),
        name=name,
    )


def power(rate, distance):
    return jnp.exp(-rate * distance)


def head_columns(h):
    return slice(h * E, (h + 1) * E)


def positions_kernel(inner):
    inner[...] = lax.broadcasted_iota(jnp.int32, inner.shape, 1).astype(F32)


def states_kernel(count, heads, inner, rates, keys, values, state, wide):
    for h in range(heads):
        rate = jnp.broadcast_to(rates[0:1, h : h + 1], (8, E))
        wide[h] = rate
        long_rate = jnp.concatenate([rate[0:1]] * (BLOCK // E), axis=1)
        scale = power(long_rate, BLOCK - 1.0 - inner[0:1])
        decay = power(rate[0:1], float(BLOCK))
        total = None
        for b in range(count):
            rows = pl.ds(b * BLOCK, BLOCK)
            scaled = keys[rows, head_columns(h)].T.astype(F32) * scale
            block = jnp.dot(
                scaled.astype(BF16), values[rows, head_columns(h)], preferred_element_type=F32
            )
            total = block if b == 0 else total * decay + block
        state[h] = total


def chip_kernel(length, half, wide, both, total):
    first = lax.axis_index("c") * half
    for i in range(half):
        decay = power(wide[first + i, 0:1], float(length))
        total[i] = both[0, first + i] * decay + both[1, first + i]


def scan_kernel(length, half, chips, wide, totals, prefixes):
    piece = lax.axis_index("z") * lax.axis_size("x") + lax.axis_index("x")
    h = lax.axis_index("c") * half + piece // (chips // half)
    decay = power(wide[h], 2.0 * length)
    running = jnp.zeros(totals.shape[1:], F32)
    for i in range(chips):
        prefixes[i] = running
        running = running * decay + totals[i]


def two_halves(matrix):
    high = matrix.astype(BF16)
    low = (matrix - high.astype(F32)).astype(BF16)
    return jnp.concatenate([high, low], axis=0)


def decay_mask(rate):
    row = lax.broadcasted_iota(jnp.int32, (E, E), 0)
    column = lax.broadcasted_iota(jnp.int32, (E, E), 1)
    distance = (row - column).astype(F32)
    within = jnp.where(distance >= 0, power(rate, jnp.maximum(distance, 0.0)), 0.0)
    to_row = power(rate, row.astype(F32))
    across = to_row * power(rate, (E - column[0:1]).astype(F32))
    return within, across


def decay_kernel(heads, wide, within, across, scale, key_scale):
    inner = lax.broadcasted_iota(jnp.int32, (BLOCK, E), 0).astype(F32)
    for h in range(heads):
        rate = wide[h, 0:1]
        within[h], across[h] = decay_mask(rate)
        scale[h] = power(rate, inner + 1.0)
        key_scale[h] = power(rate, BLOCK - 1.0 - inner)


def local_kernel(
    count, heads, wide, within, across, scale, key_scale, both, queries, keys, values, local, held
):
    second = lax.axis_index("c") == 1
    for h in range(heads):
        held[h] = jnp.where(second, both[0, h], 0.0)
    top, bottom = slice(0, E), slice(E, BLOCK)
    for b in range(count):
        rows = pl.ds(b * BLOCK, BLOCK)
        for h in range(heads):
            query = queries[rows, head_columns(h)]
            key = keys[rows, head_columns(h)]
            value = values[rows, head_columns(h)]
            scores = lax.dot_general(
                query, key, (((1,), (1,)), ((), ())), preferred_element_type=F32
            )
            upper = (scores[top, top] * within[h]).astype(BF16)
            left = (scores[bottom, top] * across[h]).astype(BF16)
            right = (scores[bottom, bottom] * within[h]).astype(BF16)
            weights = jnp.concatenate(
                [
                    jnp.concatenate([upper, jnp.zeros((E, E), BF16)], axis=1),
                    jnp.concatenate([left, right], axis=1),
                ],
                axis=0,
            )
            out = jnp.dot(weights, value, preferred_element_type=F32)
            doubled = jnp.concatenate([query, query], axis=1)
            carried = jnp.dot(doubled, two_halves(held[h]), preferred_element_type=F32)
            local[rows, head_columns(h)] = out + carried * scale[h]
            if b < count - 1:
                scaled = (key.astype(F32) * key_scale[h]).astype(BF16)
                block = lax.dot_general(
                    scaled, value, (((0,), (0,)), ((), ())), preferred_element_type=F32
                )
                held[h] = held[h] * power(wide[h, 0:1], float(BLOCK)) + block


def relay_kernel(mine, prefix):
    prefix[...] = mine[...]


def mix_kernel(count, heads, wide, scale, queries, local, prefix, gain, mixed, squares):
    length = float(count * BLOCK)
    second = lax.axis_index("c") == 1
    entering = []
    for h in range(heads):
        entering.append(two_halves(prefix[h] * jnp.where(second, power(wide[h, 0:1], length), 1.0)))
    for t in range(count * BLOCK // ROWS):
        rows = pl.ds(t * ROWS, ROWS)
        inner = t * ROWS % BLOCK
        block = t * ROWS // BLOCK
        total = jnp.zeros((ROWS, E), F32)
        for h in range(heads):
            query = queries[rows, head_columns(h)]
            doubled = jnp.concatenate([query, query], axis=1)
            out = jnp.dot(doubled, entering[h], preferred_element_type=F32)
            factor = scale[h, inner : inner + ROWS]
            if block > 0:
                factor = factor * power(wide[h, 0:1], float(block * BLOCK))
            out = local[rows, head_columns(h)] + out * factor
            mixed[rows, head_columns(h)] = out * gain[:, head_columns(h)]
            total = total + out * out
        for r in range(ROWS // E):
            sums = jnp.sum(total[r * E : (r + 1) * E].T, axis=0, keepdims=True)
            squares[:, t * (ROWS // E) + r, :] = jnp.broadcast_to(sums, (squares.shape[0], E))


def norm_kernel(mixed, squares, out_hbm, out, sems):
    sums = squares[0]
    for i in range(1, squares.shape[0]):
        sums = sums + squares[i]
    inverse = lax.rsqrt(sums / float(H * E) + EPSILON)
    tiles = out.shape[0] // E
    for t in range(tiles):
        rows = pl.ds(t * E, E)
        column = jnp.broadcast_to(inverse[t : t + 1, :], (E, E)).T
        for h in range(out.shape[1] // E):
            part = mixed[rows, head_columns(h)] * column
            out[rows, head_columns(h)] = part.astype(BF16)
        pltpu.make_async_copy(out.at[rows], out_hbm.at[rows], sems.at[t]).start()
    for t in range(tiles):
        rows = pl.ds(t * E, E)
        pltpu.make_async_copy(out.at[rows], out_hbm.at[rows], sems.at[t]).wait()


def body(queries, key_rows, value_rows, decay_rates, out_gain):
    length, width = queries.shape
    heads = decay_rates.shape[0]
    count = length // BLOCK
    half = heads // 2
    chips = lax.axis_size("z") * lax.axis_size("x")
    parts = lax.axis_size(HEAD)
    shape = jax.ShapeDtypeStruct

    inner = call(
        positions_kernel,
        shape((8, BLOCK), F32),
        [],
        VMEM,
        flops=DECAY_FLOPS,
        moved=DECAY_MOVED,
        name="positions",
    )()
    state, wide = call(
        functools.partial(states_kernel, count, heads),
        (shape((heads, E, E), F32), shape((heads, 8, E), F32)),
        [VMEM] * 4,
        (VMEM, VMEM),
        flops=2 * length * E * width,
        moved=4 * length * width,
        name="states",
    )(inner, decay_rates.reshape(1, heads), key_rows, value_rows)
    both = lax.all_gather(state, "c")
    total = call(
        functools.partial(chip_kernel, length, half),
        shape((half, E, E), F32),
        [VMEM, VMEM],
        VMEM,
        name="chip",
    )(wide, both)
    owned = lax.all_to_all(total.reshape(chips, -1, E), CHIPS, 0, 0, tiled=True)
    prefixes = call(
        functools.partial(scan_kernel, length, half, chips),
        shape(owned.shape, F32),
        [VMEM, VMEM],
        VMEM,
        name="scan",
    )(wide, owned)
    mine = lax.all_to_all(prefixes, CHIPS, 0, 0, tiled=True).reshape(half, E, E)
    mine = call(
        relay_kernel,
        shape(mine.shape, F32),
        [VMEM],
        VMEM,
        flops=DECAY_FLOPS,
        moved=DECAY_MOVED,
        name="relay",
    )(mine)
    prefix = lax.all_gather(mine, "c", tiled=True)
    decays = call(
        functools.partial(decay_kernel, heads),
        (
            shape((heads, E, E), F32),
            shape((heads, E, E), F32),
            shape((heads, BLOCK, E), F32),
            shape((heads, BLOCK, E), F32),
        ),
        [VMEM],
        (VMEM,) * 4,
        flops=DECAY_FLOPS,
        moved=DECAY_MOVED,
        name="decays",
    )(wide)
    local = call(
        functools.partial(local_kernel, count, heads),
        shape((length, width), F32),
        [VMEM] * 9,
        VMEM,
        [pltpu.VMEM((heads, E, E), F32)],
        room=LOCAL_ROOM,
        flops=8 * length * BLOCK * width,
        moved=10 * length * width,
        name="local",
    )(wide, *decays, both, queries, key_rows, value_rows)
    mixed, squares = call(
        functools.partial(mix_kernel, count, heads),
        (shape((length, width), F32), shape((parts, length // E, E), F32)),
        [VMEM] * 6,
        (VMEM, VMEM),
        flops=4 * length * E * width,
        moved=10 * length * width,
        name="mix",
    )(wide, decays[2], queries, local, prefix, out_gain.reshape(1, width))
    shared = lax.all_to_all(squares, HEAD, 0, 0, tiled=True)
    return call(
        norm_kernel,
        shape((length, width), BF16),
        [VMEM, VMEM],
        HBM,
        [pltpu.VMEM((length, width), BF16), pltpu.SemaphoreType.DMA((length // E,))],
        moved=6 * length * width,
        name="norm",
    )(mixed, shared)


def solution(mesh):
    torus = Mesh(mesh.devices.reshape(8, 4, 2, mesh.shape["head"]), ("z", "x", "c", "head"))
    in_specs = (P(SEQ, "head"), P(SEQ, "head"), P(SEQ, "head"), P("head"), P("head"))
    return jax.shard_map(
        body, mesh=torus, in_specs=in_specs, out_specs=P(SEQ, "head"), check_vma=False
    )
```

```python
import functools

import jax
import jax.numpy as jnp
from jax import lax
from jax.experimental import pallas as pl
from jax.experimental.pallas import tpu as pltpu
from jax.sharding import Mesh
from jax.sharding import PartitionSpec as P

H = 32
E = 128
BLOCK = 256
EPSILON = 1e-06
SEQ = ("z", "x", "c")
CHIPS = ("z", "x")
HEAD = "head"

F32 = jnp.float32
BF16 = jnp.bfloat16
VMEM_BYTES = 67043328
LOCAL_ROOM = 40 << 20
ROWS = 128
DECAY_FLOPS = 1 << 30
DECAY_MOVED = 8 << 20
VMEM = pl.BlockSpec(memory_space=pltpu.VMEM)
HBM = pl.BlockSpec(memory_space=pltpu.HBM)


def call(kernel, outs, ins, out_specs, scratch=(), room=40 << 20, flops=0, moved=0, name=None):
    return pl.pallas_call(
        kernel,
        out_shape=outs,
        in_specs=ins,
        out_specs=out_specs,
        scratch_shapes=list(scratch),
        compiler_params=pltpu.CompilerParams(vmem_limit_bytes=VMEM_BYTES - room),
        cost_estimate=pl.CostEstimate(flops=flops, bytes_accessed=moved, transcendentals=0),
        name=name,
    )


def power(rate, distance):
    return jnp.exp(-rate * distance)


def head_columns(h):
    return slice(h * E, (h + 1) * E)


def positions_kernel(inner):
    inner[...] = lax.broadcasted_iota(jnp.int32, inner.shape, 1).astype(F32)


def states_kernel(count, heads, inner, rates, keys, values, state, given, wide):
    for h in range(heads):
        rate = jnp.broadcast_to(rates[0:1, h : h + 1], (8, E))
        wide[h] = rate
        long_rate = jnp.concatenate([rate[0:1]] * (BLOCK // E), axis=1)
        scale = power(long_rate, BLOCK - 1.0 - inner[0:1])
        decay = power(rate[0:1], float(BLOCK))
        total = None
        for b in range(count):
            rows = pl.ds(b * BLOCK, BLOCK)
            scaled = keys[rows, head_columns(h)].T.astype(F32) * scale
            block = jnp.dot(
                scaled.astype(BF16), values[rows, head_columns(h)], preferred_element_type=F32
            )
            total = block if b == 0 else total * decay + block
        state[h] = total
    half = heads // 2
    first_core = lax.axis_index("c") == 0
    for i in range(half):
        given[i] = jnp.where(first_core, state[half + i], state[i])


def chip_kernel(length, half, wide, state, both, total, first):
    core = lax.axis_index("c")
    for i in range(half):
        decay = power(wide[core * half + i, 0:1], float(length))
        before = jnp.where(core == 0, state[i], both[0, i])
        first[i] = before
        total[i] = before * decay + jnp.where(core == 0, both[1, i], state[half + i])


def scan_kernel(length, half, chips, wide, totals, prefixes):
    piece = lax.axis_index("z") * lax.axis_size("x") + lax.axis_index("x")
    h = lax.axis_index("c") * half + piece // (chips // half)
    decay = power(wide[h], 2.0 * length)
    running = jnp.zeros(totals.shape[1:], F32)
    for i in range(chips):
        prefixes[i] = running
        running = running * decay + totals[i]


def two_halves(matrix):
    high = matrix.astype(BF16)
    low = (matrix - high.astype(F32)).astype(BF16)
    return jnp.concatenate([high, low], axis=0)


def decay_mask(rate):
    row = lax.broadcasted_iota(jnp.int32, (E, E), 0)
    column = lax.broadcasted_iota(jnp.int32, (E, E), 1)
    distance = (row - column).astype(F32)
    within = jnp.where(distance >= 0, power(rate, jnp.maximum(distance, 0.0)), 0.0)
    to_row = power(rate, row.astype(F32))
    across = to_row * power(rate, (E - column[0:1]).astype(F32))
    return within, across


def decay_kernel(heads, wide, within, across, scale, key_scale):
    inner = lax.broadcasted_iota(jnp.int32, (BLOCK, E), 0).astype(F32)
    for h in range(heads):
        rate = wide[h, 0:1]
        within[h], across[h] = decay_mask(rate)
        scale[h] = power(rate, inner + 1.0)
        key_scale[h] = power(rate, BLOCK - 1.0 - inner)


def local_kernel(
    count, heads, wide, within, across, scale, key_scale, queries, keys, values, local, held
):
    top, bottom = slice(0, E), slice(E, BLOCK)
    for b in range(count):
        rows = pl.ds(b * BLOCK, BLOCK)
        for h in range(heads):
            query = queries[rows, head_columns(h)]
            key = keys[rows, head_columns(h)]
            value = values[rows, head_columns(h)]
            scores = lax.dot_general(
                query, key, (((1,), (1,)), ((), ())), preferred_element_type=F32
            )
            upper = (scores[top, top] * within[h]).astype(BF16)
            left = (scores[bottom, top] * across[h]).astype(BF16)
            right = (scores[bottom, bottom] * within[h]).astype(BF16)
            weights = jnp.concatenate(
                [
                    jnp.concatenate([upper, jnp.zeros((E, E), BF16)], axis=1),
                    jnp.concatenate([left, right], axis=1),
                ],
                axis=0,
            )
            out = jnp.dot(weights, value, preferred_element_type=F32)
            if b > 0:
                doubled = jnp.concatenate([query, query], axis=1)
                carried = jnp.dot(doubled, two_halves(held[h]), preferred_element_type=F32)
                out = out + carried * scale[h]
            local[rows, head_columns(h)] = out
            if b < count - 1:
                scaled = (key.astype(F32) * key_scale[h]).astype(BF16)
                block = lax.dot_general(
                    scaled, value, (((0,), (0,)), ((), ())), preferred_element_type=F32
                )
                held[h] = held[h] * power(wide[h, 0:1], float(BLOCK)) + block if b > 0 else block


def relay_kernel(length, half, wide, mine, first, given):
    core = lax.axis_index("c")
    for i in range(half):
        decay = power(wide[i, 0:1], float(length))
        given[i] = jnp.where(core == 0, mine[i] * decay + first[i], mine[i])


def mix_kernel(count, heads, wide, scale, queries, local, mine, first, prefix, gain, mixed, squares):
    length = float(count * BLOCK)
    second = lax.axis_index("c") == 1
    half = heads // 2
    entering = []
    for h in range(half):
        entering.append(two_halves(jnp.where(second, prefix[h], mine[h])))
    for h in range(half, heads):
        decayed = mine[h - half] * power(wide[h, 0:1], length) + first[h - half]
        entering.append(two_halves(jnp.where(second, decayed, prefix[h])))
    for t in range(count * BLOCK // ROWS):
        rows = pl.ds(t * ROWS, ROWS)
        inner = t * ROWS % BLOCK
        block = t * ROWS // BLOCK
        total = jnp.zeros((ROWS, E), F32)
        for h in range(heads):
            query = queries[rows, head_columns(h)]
            doubled = jnp.concatenate([query, query], axis=1)
            out = jnp.dot(doubled, entering[h], preferred_element_type=F32)
            factor = scale[h, inner : inner + ROWS]
            if block > 0:
                factor = factor * power(wide[h, 0:1], float(block * BLOCK))
            out = local[rows, head_columns(h)] + out * factor
            mixed[rows, head_columns(h)] = out * gain[:, head_columns(h)]
            total = total + out * out
        for r in range(ROWS // E):
            sums = jnp.sum(total[r * E : (r + 1) * E].T, axis=0, keepdims=True)
            squares[:, t * (ROWS // E) + r, :] = jnp.broadcast_to(sums, (squares.shape[0], E))


def norm_kernel(mixed, squares, out_hbm, out, sems):
    sums = squares[0]
    for i in range(1, squares.shape[0]):
        sums = sums + squares[i]
    inverse = lax.rsqrt(sums / float(H * E) + EPSILON)
    tiles = out.shape[0] // E
    for t in range(tiles):
        rows = pl.ds(t * E, E)
        column = jnp.broadcast_to(inverse[t : t + 1, :], (E, E)).T
        for h in range(out.shape[1] // E):
            part = mixed[rows, head_columns(h)] * column
            out[rows, head_columns(h)] = part.astype(BF16)
        pltpu.make_async_copy(out.at[rows], out_hbm.at[rows], sems.at[t]).start()
    for t in range(tiles):
        rows = pl.ds(t * E, E)
        pltpu.make_async_copy(out.at[rows], out_hbm.at[rows], sems.at[t]).wait()


def body(queries, key_rows, value_rows, decay_rates, out_gain):
    length, width = queries.shape
    heads = decay_rates.shape[0]
    count = length // BLOCK
    half = heads // 2
    chips = lax.axis_size("z") * lax.axis_size("x")
    parts = lax.axis_size(HEAD)
    shape = jax.ShapeDtypeStruct

    inner = call(
        positions_kernel,
        shape((8, BLOCK), F32),
        [],
        VMEM,
        flops=DECAY_FLOPS,
        moved=DECAY_MOVED,
        name="positions",
    )()
    state, given, wide = call(
        functools.partial(states_kernel, count, heads),
        (shape((heads, E, E), F32), shape((half, E, E), F32), shape((heads, 8, E), F32)),
        [VMEM] * 4,
        (VMEM,) * 3,
        flops=2 * length * E * width,
        moved=4 * length * width,
        name="states",
    )(inner, decay_rates.reshape(1, heads), key_rows, value_rows)
    both = lax.all_gather(given, "c")
    total, first = call(
        functools.partial(chip_kernel, length, half),
        (shape((half, E, E), F32), shape((half, E, E), F32)),
        [VMEM] * 3,
        (VMEM, VMEM),
        name="chip",
    )(wide, state, both)
    owned = lax.all_to_all(total.reshape(chips, -1, E), CHIPS, 0, 0, tiled=True)
    prefixes = call(
        functools.partial(scan_kernel, length, half, chips),
        shape(owned.shape, F32),
        [VMEM, VMEM],
        VMEM,
        name="scan",
    )(wide, owned)
    mine = lax.all_to_all(prefixes, CHIPS, 0, 0, tiled=True).reshape(half, E, E)
    given = call(
        functools.partial(relay_kernel, length, half),
        shape(mine.shape, F32),
        [VMEM] * 3,
        VMEM,
        flops=DECAY_FLOPS,
        moved=DECAY_MOVED,
        name="relay",
    )(wide, mine, first)
    prefix = lax.all_gather(given, "c", tiled=True)
    decays = call(
        functools.partial(decay_kernel, heads),
        (
            shape((heads, E, E), F32),
            shape((heads, E, E), F32),
            shape((heads, BLOCK, E), F32),
            shape((heads, BLOCK, E), F32),
        ),
        [VMEM],
        (VMEM,) * 4,
        flops=DECAY_FLOPS,
        moved=DECAY_MOVED,
        name="decays",
    )(wide)
    local = call(
        functools.partial(local_kernel, count, heads),
        shape((length, width), F32),
        [VMEM] * 8,
        VMEM,
        [pltpu.VMEM((heads, E, E), F32)],
        room=LOCAL_ROOM,
        flops=8 * length * BLOCK * width,
        moved=10 * length * width,
        name="local",
    )(wide, *decays, queries, key_rows, value_rows)
    mixed, squares = call(
        functools.partial(mix_kernel, count, heads),
        (shape((length, width), F32), shape((parts, length // E, E), F32)),
        [VMEM] * 8,
        (VMEM, VMEM),
        flops=4 * length * E * width,
        moved=10 * length * width,
        name="mix",
    )(wide, decays[2], queries, local, mine, first, prefix, out_gain.reshape(1, width))
    shared = lax.all_to_all(squares, HEAD, 0, 0, tiled=True)
    return call(
        norm_kernel,
        shape((length, width), BF16),
        [VMEM, VMEM],
        HBM,
        [pltpu.VMEM((length, width), BF16), pltpu.SemaphoreType.DMA((length // E,))],
        moved=6 * length * width,
        name="norm",
    )(mixed, shared)


def solution(mesh):
    torus = Mesh(mesh.devices.reshape(8, 4, 2, mesh.shape["head"]), ("z", "x", "c", "head"))
    in_specs = (P(SEQ, "head"), P(SEQ, "head"), P(SEQ, "head"), P("head"), P("head"))
    return jax.shard_map(
        body, mesh=torus, in_specs=in_specs, out_specs=P(SEQ, "head"), check_vma=False
    )
```

```python
import functools

import jax
import jax.numpy as jnp
from jax import lax
from jax.experimental import pallas as pl
from jax.experimental.pallas import tpu as pltpu
from jax.sharding import Mesh
from jax.sharding import PartitionSpec as P

H = 32
E = 128
BLOCK = 256
EPSILON = 1e-06
SEQ = ("z", "x", "c")
CHIPS = ("z", "x")
HEAD = "head"

F32 = jnp.float32
BF16 = jnp.bfloat16
VMEM_BYTES = 67043328
LOCAL_ROOM = 40 << 20
ROWS = 128
PARTS = 4
DECAY_FLOPS = 1 << 30
DECAY_MOVED = 8 << 20
VMEM = pl.BlockSpec(memory_space=pltpu.VMEM)
HBM = pl.BlockSpec(memory_space=pltpu.HBM)


def call(kernel, outs, ins, out_specs, scratch=(), room=40 << 20, flops=0, moved=0, name=None):
    return pl.pallas_call(
        kernel,
        out_shape=outs,
        in_specs=ins,
        out_specs=out_specs,
        scratch_shapes=list(scratch),
        compiler_params=pltpu.CompilerParams(vmem_limit_bytes=VMEM_BYTES - room),
        cost_estimate=pl.CostEstimate(flops=flops, bytes_accessed=moved, transcendentals=0),
        name=name,
    )


def power(rate, distance):
    return jnp.exp(-rate * distance)


def head_columns(h):
    return slice(h * E, (h + 1) * E)


def positions_kernel(inner):
    inner[...] = lax.broadcasted_iota(jnp.int32, inner.shape, 1).astype(F32)


def keys_kernel(count, heads, inner, rates, keys, scaled, wide):
    for h in range(heads):
        rate = jnp.broadcast_to(rates[0:1, h : h + 1], (8, E))
        wide[h] = rate
        long_rate = jnp.concatenate([rate[0:1]] * (BLOCK // E), axis=1)
        scale = power(long_rate, BLOCK - 1.0 - inner[0:1])
        for b in range(count):
            rows = pl.ds(b * BLOCK, BLOCK)
            turned = keys[rows, head_columns(h)].T.astype(F32) * scale
            scaled[h, :, b * BLOCK : (b + 1) * BLOCK] = turned.astype(BF16)


def states_kernel(count, heads, wide, scaled, values, state, given):
    for h in range(heads):
        decay = power(wide[h, 0:1], float(BLOCK))
        total = None
        for b in range(count):
            rows = pl.ds(b * BLOCK, BLOCK)
            block = jnp.dot(
                scaled[h, :, b * BLOCK : (b + 1) * BLOCK],
                values[rows, head_columns(h)],
                preferred_element_type=F32,
            )
            total = block if b == 0 else total * decay + block
        state[h] = total
    half = heads // 2
    first_core = lax.axis_index("c") == 0
    for i in range(half):
        given[i] = jnp.where(first_core, state[half + i], state[i])


def chip_kernel(length, half, wide, state, both, total, first):
    core = lax.axis_index("c")
    for i in range(half):
        decay = power(wide[core * half + i, 0:1], float(length))
        before = jnp.where(core == 0, state[i], both[0, i])
        first[i] = before
        total[i] = before * decay + jnp.where(core == 0, both[1, i], state[half + i])


def scan_kernel(length, half, chips, wide, totals, prefixes_hbm, prefixes, sems):
    piece = lax.axis_index("z") * lax.axis_size("x") + lax.axis_index("x")
    h = lax.axis_index("c") * half + piece // (chips // half)
    decay = power(wide[h], 2.0 * length)
    running = jnp.zeros(totals.shape[1:], F32)

    def copy(part):
        pieces = pl.ds(part * (chips // PARTS), chips // PARTS)
        return pltpu.make_async_copy(prefixes.at[pieces], prefixes_hbm.at[pieces], sems.at[part])

    for i in range(chips):
        prefixes[i] = running
        running = running * decay + totals[i]
        if (i + 1) % (chips // PARTS) == 0:
            copy(i // (chips // PARTS)).start()
    for part in range(PARTS):
        copy(part).wait()


def two_halves(matrix):
    high = matrix.astype(BF16)
    low = (matrix - high.astype(F32)).astype(BF16)
    return jnp.concatenate([high, low], axis=0)


def decay_mask(rate):
    row = lax.broadcasted_iota(jnp.int32, (E, E), 0)
    column = lax.broadcasted_iota(jnp.int32, (E, E), 1)
    distance = (row - column).astype(F32)
    within = jnp.where(distance >= 0, power(rate, jnp.maximum(distance, 0.0)), 0.0)
    to_row = power(rate, row.astype(F32))
    across = to_row * power(rate, (E - column[0:1]).astype(F32))
    return within, across


def decay_kernel(heads, wide, within, across, scale, key_scale):
    inner = lax.broadcasted_iota(jnp.int32, (BLOCK, E), 0).astype(F32)
    for h in range(heads):
        rate = wide[h, 0:1]
        within[h], across[h] = decay_mask(rate)
        scale[h] = power(rate, inner + 1.0)
        key_scale[h] = power(rate, BLOCK - 1.0 - inner)


def local_kernel(
    count, heads, wide, within, across, scale, key_scale, queries, keys, values, local, held
):
    top, bottom = slice(0, E), slice(E, BLOCK)
    for b in range(count):
        rows = pl.ds(b * BLOCK, BLOCK)
        for h in range(heads):
            query = queries[rows, head_columns(h)]
            key = keys[rows, head_columns(h)]
            value = values[rows, head_columns(h)]
            scores = lax.dot_general(
                query, key, (((1,), (1,)), ((), ())), preferred_element_type=F32
            )
            upper = (scores[top, top] * within[h]).astype(BF16)
            left = (scores[bottom, top] * across[h]).astype(BF16)
            right = (scores[bottom, bottom] * within[h]).astype(BF16)
            weights = jnp.concatenate(
                [
                    jnp.concatenate([upper, jnp.zeros((E, E), BF16)], axis=1),
                    jnp.concatenate([left, right], axis=1),
                ],
                axis=0,
            )
            out = jnp.dot(weights, value, preferred_element_type=F32)
            if b > 0:
                doubled = jnp.concatenate([query, query], axis=1)
                carried = jnp.dot(doubled, two_halves(held[h]), preferred_element_type=F32)
                out = out + carried * scale[h]
            local[rows, head_columns(h)] = out
            if b < count - 1:
                scaled = (key.astype(F32) * key_scale[h]).astype(BF16)
                block = lax.dot_general(
                    scaled, value, (((0,), (0,)), ((), ())), preferred_element_type=F32
                )
                held[h] = held[h] * power(wide[h, 0:1], float(BLOCK)) + block if b > 0 else block


def relay_kernel(length, half, wide, mine, first, given):
    core = lax.axis_index("c")
    for i in range(half):
        decay = power(wide[i, 0:1], float(length))
        given[i] = jnp.where(core == 0, mine[i] * decay + first[i], mine[i])


def mix_kernel(count, heads, wide, scale, queries, local, mine, first, prefix, gain, mixed, squares):
    length = float(count * BLOCK)
    second = lax.axis_index("c") == 1
    half = heads // 2
    entering = []
    for h in range(half):
        entering.append(two_halves(jnp.where(second, prefix[h], mine[h])))
    for h in range(half, heads):
        decayed = mine[h - half] * power(wide[h, 0:1], length) + first[h - half]
        entering.append(two_halves(jnp.where(second, decayed, prefix[h])))
    for t in range(count * BLOCK // ROWS):
        rows = pl.ds(t * ROWS, ROWS)
        inner = t * ROWS % BLOCK
        block = t * ROWS // BLOCK
        total = jnp.zeros((ROWS, E), F32)
        for h in range(heads):
            query = queries[rows, head_columns(h)]
            doubled = jnp.concatenate([query, query], axis=1)
            out = jnp.dot(doubled, entering[h], preferred_element_type=F32)
            factor = scale[h, inner : inner + ROWS]
            if block > 0:
                factor = factor * power(wide[h, 0:1], float(block * BLOCK))
            out = local[rows, head_columns(h)] + out * factor
            mixed[rows, head_columns(h)] = out * gain[:, head_columns(h)]
            total = total + out * out
        for r in range(ROWS // E):
            sums = jnp.sum(total[r * E : (r + 1) * E].T, axis=0, keepdims=True)
            squares[:, t * (ROWS // E) + r, :] = jnp.broadcast_to(sums, (squares.shape[0], E))


def norm_kernel(mixed, squares, out_hbm, out, sems):
    sums = squares[0]
    for i in range(1, squares.shape[0]):
        sums = sums + squares[i]
    inverse = lax.rsqrt(sums / float(H * E) + EPSILON)
    tiles = out.shape[0] // E
    for t in range(tiles):
        rows = pl.ds(t * E, E)
        column = jnp.broadcast_to(inverse[t : t + 1, :], (E, E)).T
        for h in range(out.shape[1] // E):
            part = mixed[rows, head_columns(h)] * column
            out[rows, head_columns(h)] = part.astype(BF16)
        pltpu.make_async_copy(out.at[rows], out_hbm.at[rows], sems.at[t]).start()
    for t in range(tiles):
        rows = pl.ds(t * E, E)
        pltpu.make_async_copy(out.at[rows], out_hbm.at[rows], sems.at[t]).wait()


def body(queries, key_rows, value_rows, decay_rates, out_gain):
    length, width = queries.shape
    heads = decay_rates.shape[0]
    count = length // BLOCK
    half = heads // 2
    chips = lax.axis_size("z") * lax.axis_size("x")
    parts = lax.axis_size(HEAD)
    shape = jax.ShapeDtypeStruct

    inner = call(
        positions_kernel,
        shape((8, BLOCK), F32),
        [],
        VMEM,
        flops=DECAY_FLOPS,
        moved=DECAY_MOVED,
        name="positions",
    )()
    scaled, wide = call(
        functools.partial(keys_kernel, count, heads),
        (shape((heads, E, length), BF16), shape((heads, 8, E), F32)),
        [VMEM] * 3,
        (VMEM, VMEM),
        flops=2 * length * E * width,
        moved=4 * length * width,
        name="keys",
    )(inner, decay_rates.reshape(1, heads), key_rows)
    state, given = call(
        functools.partial(states_kernel, count, heads),
        (shape((heads, E, E), F32), shape((half, E, E), F32)),
        [VMEM] * 3,
        (VMEM, VMEM),
        flops=2 * length * E * width,
        moved=4 * length * width,
        name="states",
    )(wide, scaled, value_rows)
    both = lax.all_gather(given, "c")
    total, first = call(
        functools.partial(chip_kernel, length, half),
        (shape((half, E, E), F32), shape((half, E, E), F32)),
        [VMEM] * 3,
        (VMEM, VMEM),
        name="chip",
    )(wide, state, both)
    owned = lax.all_to_all(total.reshape(chips, -1, E), CHIPS, 0, 0, tiled=True)
    prefixes = call(
        functools.partial(scan_kernel, length, half, chips),
        shape(owned.shape, F32),
        [VMEM, VMEM],
        HBM,
        [pltpu.VMEM(owned.shape, F32), pltpu.SemaphoreType.DMA((PARTS,))],
        name="scan",
    )(wide, owned)
    mine = lax.all_to_all(prefixes, CHIPS, 0, 0, tiled=True).reshape(half, E, E)
    given = call(
        functools.partial(relay_kernel, length, half),
        shape(mine.shape, F32),
        [VMEM] * 3,
        VMEM,
        flops=DECAY_FLOPS,
        moved=DECAY_MOVED,
        name="relay",
    )(wide, mine, first)
    prefix = lax.all_gather(given, "c", tiled=True)
    decays = call(
        functools.partial(decay_kernel, heads),
        (
            shape((heads, E, E), F32),
            shape((heads, E, E), F32),
            shape((heads, BLOCK, E), F32),
            shape((heads, BLOCK, E), F32),
        ),
        [VMEM],
        (VMEM,) * 4,
        flops=DECAY_FLOPS,
        moved=DECAY_MOVED,
        name="decays",
    )(wide)
    local = call(
        functools.partial(local_kernel, count, heads),
        shape((length, width), F32),
        [VMEM] * 8,
        VMEM,
        [pltpu.VMEM((heads, E, E), F32)],
        room=LOCAL_ROOM,
        flops=8 * length * BLOCK * width,
        moved=10 * length * width,
        name="local",
    )(wide, *decays, queries, key_rows, value_rows)
    mixed, squares = call(
        functools.partial(mix_kernel, count, heads),
        (shape((length, width), F32), shape((parts, length // E, E), F32)),
        [VMEM] * 8,
        (VMEM, VMEM),
        flops=4 * length * E * width,
        moved=10 * length * width,
        name="mix",
    )(wide, decays[2], queries, local, mine, first, prefix, out_gain.reshape(1, width))
    shared = lax.all_to_all(squares, HEAD, 0, 0, tiled=True)
    return call(
        norm_kernel,
        shape((length, width), BF16),
        [VMEM, VMEM],
        HBM,
        [pltpu.VMEM((length, width), BF16), pltpu.SemaphoreType.DMA((length // E,))],
        moved=6 * length * width,
        name="norm",
    )(mixed, shared)


def solution(mesh):
    torus = Mesh(mesh.devices.reshape(8, 4, 2, mesh.shape["head"]), ("z", "x", "c", "head"))
    in_specs = (P(SEQ, "head"), P(SEQ, "head"), P(SEQ, "head"), P("head"), P("head"))
    return jax.shard_map(
        body, mesh=torus, in_specs=in_specs, out_specs=P(SEQ, "head"), check_vma=False
    )
```

```python
import functools

import jax
import jax.numpy as jnp
from jax import lax
from jax.experimental import pallas as pl
from jax.experimental.pallas import tpu as pltpu
from jax.sharding import Mesh
from jax.sharding import PartitionSpec as P

H = 32
E = 128
BLOCK = 256
EPSILON = 1e-06
SEQ = ("z", "x", "c")
CHIPS = ("z", "x")
HEAD = "head"

F32 = jnp.float32
BF16 = jnp.bfloat16
VMEM_BYTES = 67043328
LOCAL_ROOM = 40 << 20
ROWS = 128
DECAY_FLOPS = 1 << 30
DECAY_MOVED = 8 << 20
VMEM = pl.BlockSpec(memory_space=pltpu.VMEM)
HBM = pl.BlockSpec(memory_space=pltpu.HBM)


def call(kernel, outs, ins, out_specs, scratch=(), room=40 << 20, flops=0, moved=0, name=None):
    return pl.pallas_call(
        kernel,
        out_shape=outs,
        in_specs=ins,
        out_specs=out_specs,
        scratch_shapes=list(scratch),
        compiler_params=pltpu.CompilerParams(vmem_limit_bytes=VMEM_BYTES - room),
        cost_estimate=pl.CostEstimate(flops=flops, bytes_accessed=moved, transcendentals=0),
        name=name,
    )


def power(rate, distance):
    return jnp.exp(-rate * distance)


def head_columns(h):
    return slice(h * E, (h + 1) * E)


def positions_kernel(inner):
    inner[...] = lax.broadcasted_iota(jnp.int32, inner.shape, 1).astype(F32)


def states_kernel(count, heads, inner, rates, keys, values, state, wide):
    for h in range(heads):
        rate = jnp.broadcast_to(rates[0:1, h : h + 1], (8, E))
        wide[h] = rate
        long_rate = jnp.concatenate([rate[0:1]] * (BLOCK // E), axis=1)
        scale = power(long_rate, BLOCK - 1.0 - inner[0:1])
        decay = power(rate[0:1], float(BLOCK))
        total = None
        for b in range(count):
            rows = pl.ds(b * BLOCK, BLOCK)
            scaled = keys[rows, head_columns(h)].T.astype(F32) * scale
            block = jnp.dot(
                scaled.astype(BF16), values[rows, head_columns(h)], preferred_element_type=F32
            )
            total = block if b == 0 else total * decay + block
        state[h] = total


def chip_kernel(length, half, wide, both, total):
    first = lax.axis_index("c") * half
    for i in range(half):
        decay = power(wide[first + i, 0:1], float(length))
        total[i] = both[0, first + i] * decay + both[1, first + i]


def scan_kernel(length, half, chips, wide, totals, prefixes):
    piece = lax.axis_index("z") * lax.axis_size("x") + lax.axis_index("x")
    h = lax.axis_index("c") * half + piece // (chips // half)
    decay = power(wide[h], 2.0 * length)
    running = jnp.zeros(totals.shape[1:], F32)
    for i in range(chips):
        prefixes[i] = running
        running = running * decay + totals[i]


def two_halves(matrix):
    high = matrix.astype(BF16)
    low = (matrix - high.astype(F32)).astype(BF16)
    return jnp.concatenate([high, low], axis=0)


def decay_mask(rate):
    row = lax.broadcasted_iota(jnp.int32, (E, E), 0)
    column = lax.broadcasted_iota(jnp.int32, (E, E), 1)
    distance = (row - column).astype(F32)
    within = jnp.where(distance >= 0, power(rate, jnp.maximum(distance, 0.0)), 0.0)
    to_row = power(rate, row.astype(F32))
    across = to_row * power(rate, (E - column[0:1]).astype(F32))
    return within, across


def decay_kernel(heads, wide, within, across, scale, key_scale):
    inner = lax.broadcasted_iota(jnp.int32, (BLOCK, E), 0).astype(F32)
    for h in range(heads):
        rate = wide[h, 0:1]
        within[h], across[h] = decay_mask(rate)
        scale[h] = power(rate, inner + 1.0)
        key_scale[h] = power(rate, BLOCK - 1.0 - inner)


def local_kernel(
    count, heads, wide, within, across, scale, key_scale, both, queries, keys, values, local, held
):
    second = lax.axis_index("c") == 1
    for h in range(heads):
        held[h] = jnp.where(second, both[0, h], 0.0)
    top, bottom = slice(0, E), slice(E, BLOCK)
    for b in range(count):
        rows = pl.ds(b * BLOCK, BLOCK)
        for h in range(heads):
            query = queries[rows, head_columns(h)]
            key = keys[rows, head_columns(h)]
            value = values[rows, head_columns(h)]
            scores = lax.dot_general(
                query, key, (((1,), (1,)), ((), ())), preferred_element_type=F32
            )
            upper = (scores[top, top] * within[h]).astype(BF16)
            left = (scores[bottom, top] * across[h]).astype(BF16)
            right = (scores[bottom, bottom] * within[h]).astype(BF16)
            weights = jnp.concatenate(
                [
                    jnp.concatenate([upper, jnp.zeros((E, E), BF16)], axis=1),
                    jnp.concatenate([left, right], axis=1),
                ],
                axis=0,
            )
            out = jnp.dot(weights, value, preferred_element_type=F32)
            doubled = jnp.concatenate([query, query], axis=1)
            carried = jnp.dot(doubled, two_halves(held[h]), preferred_element_type=F32)
            local[rows, head_columns(h)] = out + carried * scale[h]
            if b < count - 1:
                scaled = (key.astype(F32) * key_scale[h]).astype(BF16)
                block = lax.dot_general(
                    scaled, value, (((0,), (0,)), ((), ())), preferred_element_type=F32
                )
                held[h] = held[h] * power(wide[h, 0:1], float(BLOCK)) + block


def relay_kernel(mine, prefix):
    prefix[...] = mine[...]


def mix_kernel(count, heads, wide, scale, queries, local, prefix, gain, mixed, squares):
    length = float(count * BLOCK)
    second = lax.axis_index("c") == 1
    entering = []
    for h in range(heads):
        entering.append(two_halves(prefix[h] * jnp.where(second, power(wide[h, 0:1], length), 1.0)))
    for t in range(count * BLOCK // ROWS):
        rows = pl.ds(t * ROWS, ROWS)
        inner = t * ROWS % BLOCK
        block = t * ROWS // BLOCK
        total = jnp.zeros((ROWS, E), F32)
        for h in range(heads):
            query = queries[rows, head_columns(h)]
            doubled = jnp.concatenate([query, query], axis=1)
            out = jnp.dot(doubled, entering[h], preferred_element_type=F32)
            factor = scale[h, inner : inner + ROWS]
            if block > 0:
                factor = factor * power(wide[h, 0:1], float(block * BLOCK))
            out = local[rows, head_columns(h)] + out * factor
            mixed[rows, head_columns(h)] = out * gain[:, head_columns(h)]
            total = total + out * out
        for r in range(ROWS // E):
            sums = jnp.sum(total[r * E : (r + 1) * E].T, axis=0, keepdims=True)
            squares[:, t * (ROWS // E) + r, :] = jnp.broadcast_to(sums, (squares.shape[0], E))


def norm_kernel(mixed, squares, out_hbm, out, sems):
    sums = squares[0]
    for i in range(1, squares.shape[0]):
        sums = sums + squares[i]
    inverse = lax.rsqrt(sums / float(H * E) + EPSILON)
    tiles = out.shape[0] // E
    for t in range(tiles):
        rows = pl.ds(t * E, E)
        column = jnp.broadcast_to(inverse[t : t + 1, :], (E, E)).T
        for h in range(out.shape[1] // E):
            part = mixed[rows, head_columns(h)] * column
            out[rows, head_columns(h)] = part.astype(BF16)
        if t % 2 == 1:
            pair = pl.ds((t - 1) * E, 2 * E)
            pltpu.make_async_copy(out.at[pair], out_hbm.at[pair], sems.at[t // 2]).start()
    for t in range(1, tiles, 2):
        pair = pl.ds((t - 1) * E, 2 * E)
        pltpu.make_async_copy(out.at[pair], out_hbm.at[pair], sems.at[t // 2]).wait()


def body(queries, key_rows, value_rows, decay_rates, out_gain):
    length, width = queries.shape
    heads = decay_rates.shape[0]
    count = length // BLOCK
    half = heads // 2
    chips = lax.axis_size("z") * lax.axis_size("x")
    parts = lax.axis_size(HEAD)
    shape = jax.ShapeDtypeStruct

    inner = call(
        positions_kernel,
        shape((8, BLOCK), F32),
        [],
        VMEM,
        flops=DECAY_FLOPS,
        moved=DECAY_MOVED,
        name="positions",
    )()
    state, wide = call(
        functools.partial(states_kernel, count, heads),
        (shape((heads, E, E), F32), shape((heads, 8, E), F32)),
        [VMEM] * 4,
        (VMEM, VMEM),
        flops=2 * length * E * width,
        moved=4 * length * width,
        name="states",
    )(inner, decay_rates.reshape(1, heads), key_rows, value_rows)
    both = lax.all_gather(state, "c")
    total = call(
        functools.partial(chip_kernel, length, half),
        shape((half, E, E), F32),
        [VMEM, VMEM],
        VMEM,
        name="chip",
    )(wide, both)
    owned = lax.all_to_all(total.reshape(chips, -1, E), CHIPS, 0, 0, tiled=True)
    prefixes = call(
        functools.partial(scan_kernel, length, half, chips),
        shape(owned.shape, F32),
        [VMEM, VMEM],
        VMEM,
        name="scan",
    )(wide, owned)
    mine = lax.all_to_all(prefixes, CHIPS, 0, 0, tiled=True).reshape(half, E, E)
    mine = call(
        relay_kernel,
        shape(mine.shape, F32),
        [VMEM],
        VMEM,
        flops=DECAY_FLOPS,
        moved=DECAY_MOVED,
        name="relay",
    )(mine)
    prefix = lax.all_gather(mine, "c", tiled=True)
    decays = call(
        functools.partial(decay_kernel, heads),
        (
            shape((heads, E, E), F32),
            shape((heads, E, E), F32),
            shape((heads, BLOCK, E), F32),
            shape((heads, BLOCK, E), F32),
        ),
        [VMEM],
        (VMEM,) * 4,
        flops=DECAY_FLOPS,
        moved=DECAY_MOVED,
        name="decays",
    )(wide)
    local = call(
        functools.partial(local_kernel, count, heads),
        shape((length, width), F32),
        [VMEM] * 9,
        VMEM,
        [pltpu.VMEM((heads, E, E), F32)],
        room=LOCAL_ROOM,
        flops=8 * length * BLOCK * width,
        moved=10 * length * width,
        name="local",
    )(wide, *decays, both, queries, key_rows, value_rows)
    mixed, squares = call(
        functools.partial(mix_kernel, count, heads),
        (shape((length, width), F32), shape((parts, length // E, E), F32)),
        [VMEM] * 6,
        (VMEM, VMEM),
        flops=4 * length * E * width,
        moved=10 * length * width,
        name="mix",
    )(wide, decays[2], queries, local, prefix, out_gain.reshape(1, width))
    shared = lax.all_to_all(squares, HEAD, 0, 0, tiled=True)
    return call(
        norm_kernel,
        shape((length, width), BF16),
        [VMEM, VMEM],
        HBM,
        [pltpu.VMEM((length, width), BF16), pltpu.SemaphoreType.DMA((count,))],
        moved=6 * length * width,
        name="norm",
    )(mixed, shared)


def solution(mesh):
    torus = Mesh(mesh.devices.reshape(8, 4, 2, mesh.shape["head"]), ("z", "x", "c", "head"))
    in_specs = (P(SEQ, "head"), P(SEQ, "head"), P(SEQ, "head"), P("head"), P("head"))
    return jax.shard_map(
        body, mesh=torus, in_specs=in_specs, out_specs=P(SEQ, "head"), check_vma=False
    )
```
